32 devices in a mesh: region: 8 (over y, x, core), group: 4 (over z).
Axes of the slice: x: 2, y: 2, z: 4, core: 2. Of those that a mesh axis runs over, the one named last changes fastest.
Arguments:
- ensemble: bfloat16 [8192, 512], P(('region', 'group')), may hold values from -6 to 6
- tiles: bfloat16 [2, 256, 8192], P(None, None, ('region', 'group')), may hold values from -0.09375 to 0.09375
- tile_live: int32 [2, 8], replicated, may hold values 0 or 1
- observed: float32 [2, 256], replicated, may hold values from -6 to 6
- perturb: bfloat16 [2, 256, 512], replicated, may hold values from -6 to 6
- obs_var: float32 [2, 256], replicated, may hold values from 0.5 to 4
Outputs:
- analysis: bfloat16 [8192, 512], P(('region', 'group'))
The draws below stay inside these ranges and needn't reach their ends.
All inputs are finite; a program needn't handle non-finite values. Where the reference program divides by a largest or mean magnitude, that divisor is 1e-20 or more.
Results may differ from the reference program's by a relative error of at most 0.013.
Values may be sent and summed in bfloat16 or wider, within the bound.
A program may use at most 64 MiB of HBM per device.

```python
import math
import jax
import jax.numpy as jnp
from jax import lax

VAR_DEV = 256
M = 512
P_SIZE = 256
BATCHES = 2
NEWTON = 4
REGIONS = 8
GROUPS = 4
VARS = 8192


def touch_ends(entries, rng, low, high):
    index_at = [jax.random.randint(jax.random.fold_in(rng, axis), (), 0, length) for axis, length in enumerate(entries.shape)]
    main_axis = entries.shape.index(max(entries.shape))
    neighbour = index_at[:main_axis] + [(index_at[main_axis] + 1) % entries.shape[main_axis]] + index_at[main_axis + 1:]
    return entries.at[tuple(index_at)].set(low).at[tuple(neighbour)].set(high)


def levels(rng, extent, cuts, least, high):
    level = 1.0
    for axis_at, blocks in cuts:
        draws = jax.random.uniform(jax.random.fold_in(jax.random.fold_in(rng, 6), axis_at), (blocks,), jnp.float32, least / len(cuts), high / len(cuts))
        level = level * jnp.repeat(jnp.exp(draws), extent[axis_at] // blocks).reshape((-1,) + (1,) * (len(extent) - 1 - axis_at))
    return level


def normal_values(key, dims, scale, most, split=(), kind=jnp.bfloat16):
    loudness = levels(key, dims, split, -0.22, 0.18) if split else 1.0
    drawn = jax.random.normal(key, dims, jnp.float32) * scale * loudness
    return jnp.minimum(jnp.maximum(drawn, -most), most).astype(kind)


def setup_inputs(seed: int = 0) -> dict:
    key_of = jax.random.split(jax.random.key(seed), 7)
    ensemble = normal_values(key_of[0], (VARS, M), 1.0, 6.0, ((0, 32),))
    tiles = normal_values(key_of[1], (BATCHES, P_SIZE, VARS), (VARS // 2) ** -0.5, 0.09375, ((2, 32),))
    tile_live = touch_ends((jax.random.randint(key_of[2], (BATCHES, REGIONS), 0, 2) < 1).astype(jnp.int32), jax.random.fold_in(key_of[2], 1), 0, 1)
    observed = normal_values(key_of[3], (BATCHES, P_SIZE), 1.0, 6.0, (), jnp.float32)
    perturb = normal_values(key_of[4], (BATCHES, P_SIZE, M), 1.0, 6.0)
    obs_var = jnp.clip(jnp.exp(jax.random.uniform(key_of[5], (BATCHES, P_SIZE), jnp.float32, math.log(0.5), math.log(4.0))), 0.5, 4.0)
    return dict(ensemble=ensemble, tiles=tiles, tile_live=tile_live, observed=observed, perturb=perturb, obs_var=obs_var)


def newton_weights(pred, obs_row, perturb_b, var_row):
    spread = pred - jnp.mean(pred, axis=1, keepdims=True)
    cov = jnp.dot(spread, spread.T, precision=lax.Precision.HIGHEST) / (M - 1) + jnp.diag(var_row)
    bound = jnp.max(jnp.sum(jnp.abs(cov), axis=1))
    ident = jnp.eye(P_SIZE, dtype=jnp.float32)
    approx = ident / bound
    for step in range(NEWTON):
        inner = 2.0 * ident - jnp.dot(cov, approx, precision=lax.Precision.HIGHEST)
        approx = jnp.dot(approx, inner, precision=lax.Precision.HIGHEST)
    innov = obs_row[:, None] + perturb_b.astype(jnp.float32) - pred
    weights = jnp.dot(approx, innov, precision=lax.Precision.HIGHEST).astype(jnp.bfloat16)
    return spread.astype(jnp.bfloat16), weights


def reference(ensemble, tiles, tile_live, observed, perturb, obs_var):
    state = ensemble
    for batch in range(BATCHES):
        rows = jnp.repeat(tile_live[batch], VAR_DEV * GROUPS).astype(jnp.bfloat16)
        live = state * rows[:, None]
        pred = jnp.dot(tiles[batch], live, preferred_element_type=jnp.float32)
        spread_low, weights = newton_weights(pred, observed[batch], perturb[batch], obs_var[batch])
        wide = state.astype(jnp.float32)
        anom = (wide - jnp.mean(wide, axis=1, keepdims=True)).astype(jnp.bfloat16)
        gain = (jnp.dot(anom, spread_low.T, preferred_element_type=jnp.float32) / (M - 1)).astype(jnp.bfloat16)
        state = (wide + jnp.dot(gain, weights, preferred_element_type=jnp.float32)).astype(jnp.bfloat16)
    return state
```

```python
import functools

import jax
import jax.numpy as jnp
from jax import lax
from jax.experimental import pallas as pl
from jax.experimental.pallas import tpu as pltpu
from jax.sharding import PartitionSpec as P

NEWTON = 4
CORES = 2
PIECES = 2
F32 = jnp.float32
BF16 = jnp.bfloat16
MESH = pl.DeviceIdType.MESH


def split(x):
    hi = x.astype(BF16)
    return hi, (x - hi.astype(F32)).astype(BF16)


def dot3(a, b):
    left = jnp.concatenate([a[0], a[0], a[1]], axis=1)
    right = jnp.concatenate([b[0], b[1], b[0]], axis=0)
    return jnp.dot(left, right, preferred_element_type=F32)


def dot_nt(a, b):
    return lax.dot_general(a, b, (((1,), (1,)), ((), ())), preferred_element_type=F32)


def kernel(
    region_count, group_count,
    ens_hbm, tiles_hbm, live_hbm, obs_hbm, pert_hbm, var_hbm,
    out_ref,
    ens, tiles, live, obs, pert, var,
    partial, rs_buf, z_send, z_buf, spread_buf,
    mean_part, mean_rs, mean_zsend, mean_z,
    pair_buf, half_send, half_buf,
    load_sem, rs_sem, z_sem, ag_sem, mean_sem, pair_sem, half_sem,
):
    batches, obs_count, members = pert.shape
    region = lax.axis_index("region")
    group = lax.axis_index("group")
    chunk_rows, chunk_cols = z_send.shape[1:]
    across = members // chunk_cols

    barrier = pltpu.get_barrier_semaphore()
    region_peers = [lax.rem(region + k, region_count) for k in range(1, region_count)]
    group_peers = [lax.rem(group + k, group_count) for k in range(1, group_count)]
    for peer in region_peers:
        pl.semaphore_signal(barrier, inc=1, device_id=(peer, group), device_id_type=MESH)
    for peer in group_peers:
        pl.semaphore_signal(barrier, inc=1, device_id=(region, peer), device_id_type=MESH)

    sources = [(ens_hbm, ens)]
    sources += [(tiles_hbm.at[b], tiles.at[b]) for b in range(batches)]
    sources += [(live_hbm, live), (obs_hbm, obs), (var_hbm, var)]
    sources += [(pert_hbm.at[b], pert.at[b]) for b in range(batches)]
    loads = [pltpu.make_async_copy(src, dst, load_sem.at[i]) for i, (src, dst) in enumerate(sources)]
    early, late = loads[:4 + batches], loads[4 + batches:]
    for load in early:
        load.start()

    row_at = lax.broadcasted_iota(jnp.int32, (obs_count, obs_count), 0)
    col_at = lax.broadcasted_iota(jnp.int32, (obs_count, obs_count), 1)
    on_diag = row_at == col_at
    ident = jnp.where(on_diag, 1.0, 0.0).astype(F32)

    def as_row(column):
        return jnp.sum(jnp.where(on_diag, column, 0.0), axis=0, keepdims=True)

    def as_column(row):
        return jnp.sum(jnp.where(on_diag, row, 0.0), axis=1, keepdims=True)

    piece_cols = chunk_cols // PIECES

    def chunk(ref, index, piece=None):
        rows = pl.ds(pl.multiple_of(lax.div(index, across) * chunk_rows, chunk_rows), chunk_rows)
        start, width = (0, chunk_cols) if piece is None else (piece * piece_cols, piece_cols)
        if across > 1:
            start = pl.multiple_of(lax.rem(index, across) * chunk_cols + start, piece_cols)
        return ref.at[rows, pl.ds(start, width)]

    def cols(ref, piece):
        return ref if piece is None else ref.at[..., pl.ds(piece * piece_cols, piece_cols)]

    def slot_of(b, piece):
        return b * PIECES + (piece or 0)

    def pieces_of(b):
        return range(PIECES) if b == 0 else (None,)

    def remote(src, dst, sems, where):
        return pltpu.make_async_remote_copy(
            src_ref=src, dst_ref=dst, send_sem=sems.at[0], recv_sem=sems.at[1],
            device_id=where, device_id_type=MESH,
        )

    sends = []

    def phase(sems, whole):
        everything = remote(whole, whole, sems, (region, lax.rem(group + 1, group_count)))
        sends.append(everything)
        return everything

    def local_partial(b):
        loads[1 + b].wait()
        value = jnp.dot(tiles[b], ens[...], preferred_element_type=F32)
        value = value * live_of[b:b + 1]
        mean = jnp.mean(value, axis=1, keepdims=True)
        partial[b] = (value - mean).astype(BF16)
        return mean

    chips = region_count // CORES
    chip, core = lax.div(region, CORES), lax.rem(region, CORES)
    chip_peers = [lax.rem(chip + k, chips) for k in range(1, chips)]
    partner = chip * CORES + (CORES - 1 - core)

    phases = {}

    def scatter(b, piece):
        sems = rs_sem.at[slot_of(b, piece)]
        for k, peer in enumerate(region_peers):
            remote(chunk(partial.at[b], peer, piece), cols(rs_buf.at[k], piece), sems, (peer, group)).start()
        phases["rs", b, piece] = phase(sems, cols(rs_buf, piece))

    def scatter_pair(b):
        for k, there in enumerate(chip_peers + [chip]):
            sems = pair_sem.at[b - 1, k]
            remote(chunk(partial.at[b], there * CORES + CORES - 1 - core), pair_buf.at[b - 1, k], sems, (partner, group)).start()
            phases["pair", b, k] = phase(sems, pair_buf.at[b - 1, k])

    def pair_sum(b, k, there):
        phases["pair", b, k].wait_recv()
        return chunk(partial.at[b], there * CORES + core)[...].astype(F32) + pair_buf[b - 1, k].astype(F32)

    def scatter_chips(b):
        sems = half_sem.at[b - 1]
        for k, there in enumerate(chip_peers):
            half_send[b - 1, k] = pair_sum(b, k, there).astype(BF16)
            remote(half_send.at[b - 1, k], half_buf.at[b - 1, k], sems, (there * CORES + core, group)).start()
        phases["rs", b, None] = phase(sems, half_buf.at[b - 1])

    def sum_region(b, piece):
        if b == 0:
            total, buf = chunk(partial.at[b], region, piece)[...].astype(F32), cols(rs_buf, piece)
        else:
            total, buf = pair_sum(b, chips - 1, chip), half_buf.at[b - 1]
        phases["rs", b, piece].wait_recv()
        for k in range(buf.shape[0]):
            total = total + buf[k].astype(F32)
        mine = cols(z_send.at[b], piece)
        mine[...] = total.astype(BF16)
        sems = z_sem.at[slot_of(b, piece)]
        for k, peer in enumerate(group_peers):
            remote(mine, cols(z_buf.at[b, k], piece), sems, (region, peer)).start()
        phases["z", b, piece] = phase(sems, cols(z_buf.at[b], piece))

    def sum_group(b, piece):
        total = cols(z_send.at[b], piece)[...].astype(F32)
        phases["z", b, piece].wait_recv()
        for k in range(group_count - 1):
            total = total + cols(z_buf.at[b, k], piece)[...].astype(F32)
        mine = chunk(spread_buf.at[b], region, piece)
        mine[...] = total.astype(BF16)
        sems = ag_sem.at[slot_of(b, piece)]
        for k, peer in enumerate(region_peers):
            remote(mine, mine, sems, (peer, group)).start()
        phases["ag", b, piece] = phase(sems, cols(rs_buf, piece))

    def gathered(b):
        for piece in pieces_of(b):
            phases["ag", b, piece].wait_recv()
        return spread_buf[b]

    loads[1 + batches].wait()
    region_at = lax.broadcasted_iota(jnp.int32, live.shape, 1)
    live_of = jnp.sum(jnp.where(region_at == region, live[...].astype(F32), 0.0), axis=1, keepdims=True)
    loads[0].wait()
    means = [local_partial(0)]
    pl.semaphore_wait(barrier, region_count - 1 + group_count - 1)
    for piece in pieces_of(0):
        scatter(0, piece)
    for load in late:
        load.start()
    for b in range(1, batches):
        means.append(local_partial(b))
    for b in range(1, batches):
        scatter_pair(b)
    for b in range(batches):
        mean_part[:, b * obs_count:(b + 1) * obs_count] = as_row(means[b])
    for k, peer in enumerate(region_peers):
        remote(mean_part, mean_rs.at[k], mean_sem.at[0], (peer, group)).start()
    mean_region = phase(mean_sem.at[0], mean_rs)
    for b in range(1, batches):
        scatter_chips(b)
    for piece in pieces_of(0):
        sum_region(0, piece)
    total = mean_part[...]
    mean_region.wait_recv()
    for k in range(region_count - 1):
        total = total + mean_rs[k]
    mean_zsend[...] = total
    for k, peer in enumerate(group_peers):
        remote(mean_zsend, mean_z.at[k], mean_sem.at[1], (region, peer)).start()
    mean_group = phase(mean_sem.at[1], mean_z)
    for b in range(1, batches):
        sum_region(b, None)
    for piece in pieces_of(0):
        sum_group(0, piece)
    mean_row = mean_zsend[...]
    mean_group.wait_recv()
    for k in range(group_count - 1):
        mean_row = mean_row + mean_z[k]
    for b in range(1, batches):
        sum_group(b, None)
    for load in early[2 + batches:]:
        load.wait()

    def anomaly(wide):
        return (wide - jnp.mean(wide, axis=1, keepdims=True)).astype(BF16)

    def newton_weights(spread_low, mismatch, shift, b):
        cov = dot_nt(spread_low, spread_low) / (members - 1) + jnp.where(on_diag, var[b:b + 1, :], 0.0)
        bound = jnp.max(jnp.sum(jnp.abs(cov), axis=1, keepdims=True), axis=0, keepdims=True)
        residual = ident - cov / bound
        approx = ident + residual
        for step in range(1, NEWTON):
            parts = split(residual)
            residual = dot3(parts, parts)
            approx = approx + dot3(split(approx), split(residual))
        innov = mismatch + shift
        return (dot3(split(approx), split(innov)) / bound).astype(BF16)

    state = ens[...].astype(F32)
    anom = anomaly(state)
    offsets = [
        as_column(obs[b:b + 1, :] - mean_row[:, b * obs_count:(b + 1) * obs_count]) for b in range(batches)
    ]
    history = []
    for b in range(batches):
        late[b].wait()
        prior = gathered(b)
        spread = prior.astype(F32)
        for earlier_low, earlier_weights in history:
            base = spread - jnp.mean(spread, axis=1, keepdims=True)
            hi, lo = split(base)
            cross = split((dot_nt(hi, earlier_low) + dot_nt(lo, earlier_low)) / (members - 1))
            spread = spread + jnp.dot(cross[0], earlier_weights, preferred_element_type=F32)
            spread = spread + jnp.dot(cross[1], earlier_weights, preferred_element_type=F32)
        mismatch = pert[b].astype(F32) - spread
        if history:
            spread = spread - jnp.mean(spread, axis=1, keepdims=True)
        spread_low = spread.astype(BF16)
        gain = (dot_nt(anom, spread_low) / (members - 1)).astype(BF16)
        weights = newton_weights(spread_low, mismatch, offsets[b], b)
        low = (state + jnp.dot(gain, weights, preferred_element_type=F32)).astype(BF16)
        history.append((spread_low, weights))
        if b + 1 < batches:
            state = low.astype(F32)
            anom = anomaly(state)
    out_ref[...] = low
    for copy in sends:
        copy.wait_send()


def on_device(ensemble, tiles, tile_live, observed, perturb, obs_var):
    region_count = lax.axis_size("region")
    group_count = lax.axis_size("group")
    batches, obs_count, members = perturb.shape
    chunk_rows = max(16, obs_count // region_count)
    chunk_cols = obs_count * members // (region_count * chunk_rows)
    chips = region_count // CORES
    hbm = pl.BlockSpec(memory_space=pl.ANY)
    block = (chunk_rows, chunk_cols)
    dma = pltpu.SemaphoreType.DMA
    return pl.pallas_call(
        functools.partial(kernel, region_count, group_count),
        out_shape=pltpu.VMEM(ensemble.shape, ensemble.dtype),
        in_specs=[hbm] * 6,
        out_specs=pl.BlockSpec(memory_space=pltpu.VMEM),
        scratch_shapes=[
            pltpu.VMEM(ensemble.shape, BF16),
            pltpu.VMEM(tiles.shape, BF16),
            pltpu.VMEM(tile_live.shape, tile_live.dtype),
            pltpu.VMEM(observed.shape, F32),
            pltpu.VMEM(perturb.shape, BF16),
            pltpu.VMEM(obs_var.shape, F32),
            pltpu.VMEM(perturb.shape, BF16),
            pltpu.VMEM((region_count - 1, *block), BF16),
            pltpu.VMEM((batches, *block), BF16),
            pltpu.VMEM((batches, group_count - 1, *block), BF16),
            pltpu.VMEM(perturb.shape, BF16),
            pltpu.VMEM((1, batches * obs_count), F32),
            pltpu.VMEM((region_count - 1, 1, batches * obs_count), F32),
            pltpu.VMEM((1, batches * obs_count), F32),
            pltpu.VMEM((group_count - 1, 1, batches * obs_count), F32),
            pltpu.VMEM((batches - 1, chips, *block), BF16),
            pltpu.VMEM((batches - 1, chips - 1, *block), BF16),
            pltpu.VMEM((batches - 1, chips - 1, *block), BF16),
            dma((4 + 2 * batches,)),
            dma((PIECES, 2)),
            dma((batches * PIECES, 2)),
            dma((batches * PIECES, 2)),
            dma((2, 2)),
            dma((batches - 1, chips, 2)),
            dma((batches - 1, 2)),
        ],
        compiler_params=pltpu.CompilerParams(collective_id=0, has_side_effects=True),
    )(ensemble, tiles, tile_live, observed, perturb, obs_var)


def solution(mesh):
    return jax.shard_map(
        on_device,
        mesh=mesh,
        in_specs=(
            P(("region", "group"), None),
            P(None, None, ("region", "group")),
            P(),
            P(),
            P(),
            P(),
        ),
        out_specs=P(("region", "group"), None),
        check_vma=False,
    )
```

```python
import functools

import jax
import jax.numpy as jnp
from jax import lax
from jax.experimental import pallas as pl
from jax.experimental.pallas import tpu as pltpu
from jax.sharding import PartitionSpec as P

NEWTON = 4
CORES = 2
PIECES = 2
F32 = jnp.float32
BF16 = jnp.bfloat16
MESH = pl.DeviceIdType.MESH


def dot(a, b):
    return jnp.dot(a, b, preferred_element_type=F32)


def dot_nt(a, b):
    return lax.dot_general(a, b, (((1,), (1,)), ((), ())), preferred_element_type=F32)


def kernel(
    region_count, group_count,
    ens_hbm, tiles_hbm, live_hbm, obs_hbm, pert_hbm, var_hbm,
    out_ref,
    ens, tiles, live, obs, pert, var,
    partial, rs_buf, z_send, z_buf, spread_buf,
    mean_part, mean_rs, mean_zsend, mean_z,
    pair_buf, half_send, half_buf,
    load_sem, rs_sem, z_sem, ag_sem, mean_sem, pair_sem, half_sem,
):
    batches, obs_count, members = pert.shape
    region = lax.axis_index("region")
    group = lax.axis_index("group")
    chunk_rows, chunk_cols = z_send.shape[1:]
    across = members // chunk_cols

    barrier = pltpu.get_barrier_semaphore()
    region_peers = [lax.rem(region + k, region_count) for k in range(1, region_count)]
    group_peers = [lax.rem(group + k, group_count) for k in range(1, group_count)]
    for peer in region_peers:
        pl.semaphore_signal(barrier, inc=1, device_id=(peer, group), device_id_type=MESH)
    for peer in group_peers:
        pl.semaphore_signal(barrier, inc=1, device_id=(region, peer), device_id_type=MESH)

    sources = [(ens_hbm, ens)]
    sources += [(tiles_hbm.at[b], tiles.at[b]) for b in range(batches)]
    sources += [(live_hbm, live), (obs_hbm, obs), (var_hbm, var)]
    sources += [(pert_hbm.at[b], pert.at[b]) for b in range(batches)]
    loads = [pltpu.make_async_copy(src, dst, load_sem.at[i]) for i, (src, dst) in enumerate(sources)]
    early, late = loads[:4 + batches], loads[4 + batches:]
    for load in early:
        load.start()

    row_at = lax.broadcasted_iota(jnp.int32, (obs_count, obs_count), 0)
    col_at = lax.broadcasted_iota(jnp.int32, (obs_count, obs_count), 1)
    on_diag = row_at == col_at
    ident = jnp.where(on_diag, 1.0, 0.0).astype(F32)

    def as_row(column):
        return jnp.sum(jnp.where(on_diag, column, 0.0), axis=0, keepdims=True)

    def as_column(row):
        return jnp.sum(jnp.where(on_diag, row, 0.0), axis=1, keepdims=True)

    piece_cols = chunk_cols // PIECES

    def chunk(ref, index, piece=None):
        rows = pl.ds(pl.multiple_of(lax.div(index, across) * chunk_rows, chunk_rows), chunk_rows)
        start, width = (0, chunk_cols) if piece is None else (piece * piece_cols, piece_cols)
        if across > 1:
            start = pl.multiple_of(lax.rem(index, across) * chunk_cols + start, piece_cols)
        return ref.at[rows, pl.ds(start, width)]

    def cols(ref, piece):
        return ref if piece is None else ref.at[..., pl.ds(piece * piece_cols, piece_cols)]

    def slot_of(b, piece):
        return b * PIECES + (piece or 0)

    def pieces_of(b):
        return range(PIECES) if b == 0 else (None,)

    def remote(src, dst, sems, where):
        return pltpu.make_async_remote_copy(
            src_ref=src, dst_ref=dst, send_sem=sems.at[0], recv_sem=sems.at[1],
            device_id=where, device_id_type=MESH,
        )

    sends = []

    def phase(sems, whole):
        everything = remote(whole, whole, sems, (region, lax.rem(group + 1, group_count)))
        sends.append(everything)
        return everything

    def local_partial(b):
        loads[1 + b].wait()
        value = jnp.dot(tiles[b], ens[...], preferred_element_type=F32)
        value = value * live_of[b:b + 1]
        mean = jnp.mean(value, axis=1, keepdims=True)
        partial[b] = (value - mean).astype(BF16)
        return mean

    chips = region_count // CORES
    chip, core = lax.div(region, CORES), lax.rem(region, CORES)
    chip_peers = [lax.rem(chip + k, chips) for k in range(1, chips)]
    partner = chip * CORES + (CORES - 1 - core)

    phases = {}

    def scatter(b, piece):
        sems = rs_sem.at[slot_of(b, piece)]
        for k, peer in enumerate(region_peers):
            remote(chunk(partial.at[b], peer, piece), cols(rs_buf.at[k], piece), sems, (peer, group)).start()
        phases["rs", b, piece] = phase(sems, cols(rs_buf, piece))

    def scatter_pair(b):
        for k, there in enumerate(chip_peers + [chip]):
            sems = pair_sem.at[b - 1, k]
            remote(chunk(partial.at[b], there * CORES + CORES - 1 - core), pair_buf.at[b - 1, k], sems, (partner, group)).start()
            phases["pair", b, k] = phase(sems, pair_buf.at[b - 1, k])

    def pair_sum(b, k, there):
        phases["pair", b, k].wait_recv()
        return chunk(partial.at[b], there * CORES + core)[...].astype(F32) + pair_buf[b - 1, k].astype(F32)

    def scatter_chips(b):
        sems = half_sem.at[b - 1]
        for k, there in enumerate(chip_peers):
            half_send[b - 1, k] = pair_sum(b, k, there).astype(BF16)
            remote(half_send.at[b - 1, k], half_buf.at[b - 1, k], sems, (there * CORES + core, group)).start()
        phases["rs", b, None] = phase(sems, half_buf.at[b - 1])

    def sum_region(b, piece):
        if b == 0:
            total, buf = chunk(partial.at[b], region, piece)[...].astype(F32), cols(rs_buf, piece)
        else:
            total, buf = pair_sum(b, chips - 1, chip), half_buf.at[b - 1]
        phases["rs", b, piece].wait_recv()
        for k in range(buf.shape[0]):
            total = total + buf[k].astype(F32)
        mine = cols(z_send.at[b], piece)
        mine[...] = total.astype(BF16)
        sems = z_sem.at[slot_of(b, piece)]
        for k, peer in enumerate(group_peers):
            remote(mine, cols(z_buf.at[b, k], piece), sems, (region, peer)).start()
        phases["z", b, piece] = phase(sems, cols(z_buf.at[b], piece))

    def sum_group(b, piece):
        total = cols(z_send.at[b], piece)[...].astype(F32)
        phases["z", b, piece].wait_recv()
        for k in range(group_count - 1):
            total = total + cols(z_buf.at[b, k], piece)[...].astype(F32)
        mine = chunk(spread_buf.at[b], region, piece)
        mine[...] = total.astype(BF16)
        sems = ag_sem.at[slot_of(b, piece)]
        for k, peer in enumerate(region_peers):
            remote(mine, mine, sems, (peer, group)).start()
        phases["ag", b, piece] = phase(sems, cols(rs_buf, piece))

    def gathered(b):
        for piece in pieces_of(b):
            phases["ag", b, piece].wait_recv()
        return spread_buf[b]

    loads[1 + batches].wait()
    region_at = lax.broadcasted_iota(jnp.int32, live.shape, 1)
    live_of = jnp.sum(jnp.where(region_at == region, live[...].astype(F32), 0.0), axis=1, keepdims=True)
    loads[0].wait()
    means = [local_partial(0)]
    pl.semaphore_wait(barrier, region_count - 1 + group_count - 1)
    for piece in pieces_of(0):
        scatter(0, piece)
    for load in late:
        load.start()
    for b in range(1, batches):
        means.append(local_partial(b))
    for b in range(1, batches):
        scatter_pair(b)
    for b in range(batches):
        mean_part[:, b * obs_count:(b + 1) * obs_count] = as_row(means[b])
    for k, peer in enumerate(region_peers):
        remote(mean_part, mean_rs.at[k], mean_sem.at[0], (peer, group)).start()
    mean_region = phase(mean_sem.at[0], mean_rs)
    for b in range(1, batches):
        scatter_chips(b)
    for piece in pieces_of(0):
        sum_region(0, piece)
    total = mean_part[...]
    mean_region.wait_recv()
    for k in range(region_count - 1):
        total = total + mean_rs[k]
    mean_zsend[...] = total
    for k, peer in enumerate(group_peers):
        remote(mean_zsend, mean_z.at[k], mean_sem.at[1], (region, peer)).start()
    mean_group = phase(mean_sem.at[1], mean_z)
    for b in range(1, batches):
        sum_region(b, None)
    for piece in pieces_of(0):
        sum_group(0, piece)
    mean_row = mean_zsend[...]
    mean_group.wait_recv()
    for k in range(group_count - 1):
        mean_row = mean_row + mean_z[k]
    for b in range(1, batches):
        sum_group(b, None)
    for load in early[2 + batches:]:
        load.wait()

    def anomaly(wide):
        return (wide - jnp.mean(wide, axis=1, keepdims=True)).astype(BF16)

    def newton_weights(spread, spread_low, innov, b):
        power = jnp.sum(jnp.sum(spread * spread, axis=0, keepdims=True), axis=1, keepdims=True) / (members - 1)
        centre = (power + jnp.sum(var[b:b + 1, :], axis=1, keepdims=True)) / obs_count
        cov = dot_nt(spread_low, spread_low) / (members - 1) + jnp.where(on_diag, var[b:b + 1, :], 0.0)
        rest = cov - jnp.where(on_diag, centre, 0.0)
        low = rest.astype(BF16)
        bound = jnp.max(jnp.sum(jnp.abs(cov), axis=0, keepdims=True), axis=1, keepdims=True)
        inverse = 1.0 / bound
        shift = 1.0 - centre * inverse
        square = dot(low, low)
        weights = (1.0 + shift) * innov - inverse * dot(low, innov.astype(BF16))
        rest = (inverse * inverse) * square - (2.0 * shift * inverse) * rest
        for step in range(1, NEWTON):
            shift = shift * shift
            low = rest.astype(BF16)
            weights, square = (1.0 + shift) * weights + dot(low, weights.astype(BF16)), dot(low, low)
            rest = square + (2.0 * shift) * rest
        return (weights * inverse).astype(BF16)

    state = ens[...].astype(F32)
    anom = anomaly(state)
    offsets = [
        as_column(obs[b:b + 1, :] - mean_row[:, b * obs_count:(b + 1) * obs_count]) for b in range(batches)
    ]
    history = []
    for b in range(batches):
        late[b].wait()
        prior = gathered(b)
        spread = prior.astype(F32)
        mismatch = pert[b].astype(F32) - spread
        for earlier_low, earlier_weights in history:
            cross = (dot_nt(spread.astype(BF16), earlier_low) / (members - 1)).astype(BF16)
            change = dot(cross, earlier_weights)
            mismatch = mismatch - change
            spread = spread + (change - jnp.mean(change, axis=1, keepdims=True))
        spread_low = spread.astype(BF16)
        gain = (dot_nt(anom, spread_low) / (members - 1)).astype(BF16)
        weights = newton_weights(spread, spread_low, mismatch + offsets[b], b)
        low = (state + dot(gain, weights)).astype(BF16)
        history.append((spread_low, weights))
        if b + 1 < batches:
            state = low.astype(F32)
            anom = anomaly(state)
    out_ref[...] = low
    for copy in sends:
        copy.wait_send()


def on_device(ensemble, tiles, tile_live, observed, perturb, obs_var):
    region_count = lax.axis_size("region")
    group_count = lax.axis_size("group")
    batches, obs_count, members = perturb.shape
    chunk_rows = max(16, obs_count // region_count)
    chunk_cols = obs_count * members // (region_count * chunk_rows)
    chips = region_count // CORES
    hbm = pl.BlockSpec(memory_space=pl.ANY)
    block = (chunk_rows, chunk_cols)
    dma = pltpu.SemaphoreType.DMA
    return pl.pallas_call(
        functools.partial(kernel, region_count, group_count),
        out_shape=pltpu.VMEM(ensemble.shape, ensemble.dtype),
        in_specs=[hbm] * 6,
        out_specs=pl.BlockSpec(memory_space=pltpu.VMEM),
        scratch_shapes=[
            pltpu.VMEM(ensemble.shape, BF16),
            pltpu.VMEM(tiles.shape, BF16),
            pltpu.VMEM(tile_live.shape, tile_live.dtype),
            pltpu.VMEM(observed.shape, F32),
            pltpu.VMEM(perturb.shape, BF16),
            pltpu.VMEM(obs_var.shape, F32),
            pltpu.VMEM(perturb.shape, BF16),
            pltpu.VMEM((region_count - 1, *block), BF16),
            pltpu.VMEM((batches, *block), BF16),
            pltpu.VMEM((batches, group_count - 1, *block), BF16),
            pltpu.VMEM(perturb.shape, BF16),
            pltpu.VMEM((1, batches * obs_count), F32),
            pltpu.VMEM((region_count - 1, 1, batches * obs_count), F32),
            pltpu.VMEM((1, batches * obs_count), F32),
            pltpu.VMEM((group_count - 1, 1, batches * obs_count), F32),
            pltpu.VMEM((batches - 1, chips, *block), BF16),
            pltpu.VMEM((batches - 1, chips - 1, *block), BF16),
            pltpu.VMEM((batches - 1, chips - 1, *block), BF16),
            dma((4 + 2 * batches,)),
            dma((PIECES, 2)),
            dma((batches * PIECES, 2)),
            dma((batches * PIECES, 2)),
            dma((2, 2)),
            dma((batches - 1, chips, 2)),
            dma((batches - 1, 2)),
        ],
        compiler_params=pltpu.CompilerParams(collective_id=0, has_side_effects=True),
    )(ensemble, tiles, tile_live, observed, perturb, obs_var)


def solution(mesh):
    return jax.shard_map(
        on_device,
        mesh=mesh,
        in_specs=(
            P(("region", "group"), None),
            P(None, None, ("region", "group")),
            P(),
            P(),
            P(),
            P(),
        ),
        out_specs=P(("region", "group"), None),
        check_vma=False,
    )
```

```python
import functools

import jax
import jax.numpy as jnp
from jax import lax
from jax.experimental import pallas as pl
from jax.experimental.pallas import tpu as pltpu
from jax.sharding import PartitionSpec as P

NEWTON = 4
CORES = 2
PLANES = 2
F32 = jnp.float32
BF16 = jnp.bfloat16
MESH = pl.DeviceIdType.MESH


def dot(a, b):
    return jnp.dot(a, b, preferred_element_type=F32)


def dot_nt(a, b):
    return lax.dot_general(a, b, (((1,), (1,)), ((), ())), preferred_element_type=F32)


def dot_tn(a, b):
    return lax.dot_general(a, b, (((0,), (0,)), ((), ())), preferred_element_type=F32)


def parts_of(batch, chunk_cols):
    half = chunk_cols // 2
    if batch == 0 and half % 128 == 0:
        return [(0, half, False, True), (half, half, True, False)]
    return [(0, chunk_cols, batch > 0, False)]


def kernel(
    region_count, group_count,
    ens_hbm, tiles_hbm, live_hbm, obs_hbm, pert_hbm, var_hbm,
    out_ref,
    ens, tiles, live, obs, pert, var,
    partial, direct, pair, half_send, half, z_send, z_buf, spread_buf,
    mean_part, mean_rs, mean_zsend, mean_z, all_sent,
    load_sem, send_sem, rs_sem, pair_sem, z_sem, ag_sem, hop_sem, mean_sem,
):
    batches, obs_count, members = pert.shape
    owners, chunk_rows, chunk_cols = partial.shape[1:]
    across = members // chunk_cols
    blocks = owners // across
    planes = owners // region_count
    sites = owners // CORES
    region = lax.axis_index("region")
    group = lax.axis_index("group")
    high, plane = lax.div(group, planes), lax.rem(group, planes)
    mine = plane * region_count + region
    site, core = lax.div(mine, CORES), lax.rem(mine, CORES)

    def others(me, count):
        peers = [k + (me <= k).astype(jnp.int32) for k in range(count - 1)]
        return [(peer, me - (me > peer).astype(jnp.int32)) for peer in peers]

    def device(owner):
        return lax.rem(owner, region_count), high * planes + lax.div(owner, region_count)

    near = others(mine, owners)
    near_sites = others(site, sites)
    far = [((region, there * planes + plane), slot) for there, slot in others(high, group_count // planes)]
    partner = device(site * CORES + CORES - 1 - core)

    barrier = pltpu.get_barrier_semaphore()
    for owner, _ in near:
        pl.semaphore_signal(barrier, inc=1, device_id=device(owner), device_id_type=MESH)
    for where, _ in far:
        pl.semaphore_signal(barrier, inc=1, device_id=where, device_id_type=MESH)

    sources = [(ens_hbm, ens)]
    sources += [(tiles_hbm.at[b], tiles.at[b]) for b in range(batches)]
    sources += [(live_hbm, live), (obs_hbm, obs), (var_hbm, var)]
    sources += [(pert_hbm.at[b], pert.at[b]) for b in range(batches)]
    loads = [pltpu.make_async_copy(src, dst, load_sem.at[i]) for i, (src, dst) in enumerate(sources)]
    early, late = loads[:4 + batches], loads[4 + batches:]
    for load in early:
        load.start()

    row_at = lax.broadcasted_iota(jnp.int32, (obs_count, obs_count), 0)
    col_at = lax.broadcasted_iota(jnp.int32, (obs_count, obs_count), 1)
    on_diag = row_at == col_at

    def as_row(column):
        return jnp.sum(jnp.where(on_diag, column, 0.0), axis=0, keepdims=True)

    def as_column(row):
        return jnp.sum(jnp.where(on_diag, row, 0.0), axis=1, keepdims=True)

    def remote(src, dst, recv_sem, where):
        return pltpu.make_async_remote_copy(
            src_ref=src, dst_ref=dst, send_sem=send_sem, recv_sem=recv_sem,
            device_id=where, device_id_type=MESH,
        )

    def arrived(ref, recv_sem):
        remote(ref, ref, recv_sem, partner).wait_recv()

    parts = [(b, *part) for b in range(batches) for part in parts_of(b, chunk_cols)]

    def cols(ref, part):
        return ref.at[..., pl.ds(parts[part][1], parts[part][2])]

    def of_batch(b):
        return [i for i, part in enumerate(parts) if part[0] == b]

    def local_partial(b):
        loads[1 + b].wait()
        value = dot(tiles[b], ens[...]) * live_of[b:b + 1]
        mean = jnp.mean(value, axis=1, keepdims=True)
        value = (value - mean).astype(BF16)
        for a in range(across):
            block = value[:, a * chunk_cols:(a + 1) * chunk_cols]
            partial[b, a * blocks:(a + 1) * blocks] = block.reshape(blocks, chunk_rows, chunk_cols)
        return mean

    def scatter_direct(i):
        b = parts[i][0]
        for owner, slot in near[::-1]:
            remote(cols(partial.at[b, owner], i), cols(direct.at[slot], i), rs_sem.at[i], device(owner)).start()

    def scatter_pair(i):
        b = parts[i][0]
        for k in range(sites):
            src = cols(partial.at[b, k * CORES + CORES - 1 - core], i)
            remote(src, cols(pair.at[b, k], i), pair_sem.at[i], partner).start()

    def scatter_sites(i):
        b = parts[i][0]
        arrived(cols(pair.at[b], i), pair_sem.at[i])
        for k, (there, slot) in list(enumerate(near_sites))[::-1]:
            total = cols(partial.at[b, there * CORES + core], i)[...].astype(F32) + cols(pair.at[b, there], i)[...].astype(F32)
            cols(half_send.at[b, k], i)[...] = total.astype(BF16)
            where = device(there * CORES + core)
            remote(cols(half_send.at[b, k], i), cols(half.at[b, slot], i), rs_sem.at[i], where).start()

    def sum_near(i):
        b = parts[i][0]
        total = cols(partial.at[b, mine], i)[...].astype(F32)
        if parts[i][3]:
            total = total + cols(pair.at[b, site], i)[...].astype(F32)
            arrivals = cols(half.at[b], i)
        else:
            arrivals = cols(direct, i)
        arrived(arrivals, rs_sem.at[i])
        for k in range(arrivals.shape[0]):
            total = total + arrivals[k].astype(F32)
        cols(z_send.at[b], i)[...] = total.astype(BF16)
        for where, slot in far:
            remote(cols(z_send.at[b], i), cols(z_buf.at[b, slot], i), z_sem.at[i], where).start()

    def sum_far(i):
        b = parts[i][0]
        total = cols(z_send.at[b], i)[...].astype(F32)
        arrived(cols(z_buf.at[b], i), z_sem.at[i])
        for k in range(len(far)):
            total = total + cols(z_buf.at[b, k], i)[...].astype(F32)
        ours = cols(spread_buf.at[b, mine], i)
        ours[...] = total.astype(BF16)
        if not parts[i][4]:
            for owner, _ in near:
                remote(ours, ours, ag_sem.at[i], device(owner)).start()
            return
        for there in range(sites // planes * (planes - 1)):
            owner = (there + jnp.where(there >= plane * (sites // planes), sites // planes, 0)) * CORES + core
            remote(ours, ours, hop_sem.at[0, i], device(owner)).start()
        for peer, _ in others(region, region_count):
            remote(ours, ours, ag_sem.at[i], device(plane * region_count + peer)).start()

    def pass_on(i):
        count = sites // planes * (planes - 1)
        arrived(cols(direct.at[pl.ds(0, count)], i), hop_sem.at[0, i])
        for there in range(count):
            owner = (there + jnp.where(there >= plane * (sites // planes), sites // planes, 0)) * CORES + core
            block = cols(spread_buf.at[parts[i][0], owner], i)
            remote(block, block, hop_sem.at[1, i], partner).start()

    def gathered(b):
        for i in of_batch(b):
            if parts[i][4]:
                arrived(cols(direct.at[pl.ds(0, sites // planes * (planes - 1))], i), hop_sem.at[1, i])
                arrived(cols(direct.at[pl.ds(0, region_count - 1)], i), ag_sem.at[i])
            else:
                arrived(cols(direct, i), ag_sem.at[i])
        blocks_of = [spread_buf[b, a * blocks:(a + 1) * blocks].reshape(obs_count, chunk_cols) for a in range(across)]
        return jnp.concatenate(blocks_of, axis=1) if across > 1 else blocks_of[0]

    loads[1 + batches].wait()
    region_at = lax.broadcasted_iota(jnp.int32, live.shape, 1)
    live_of = jnp.sum(jnp.where(region_at == region, live[...].astype(F32), 0.0), axis=1, keepdims=True)
    loads[0].wait()
    means = [local_partial(0)]
    pl.semaphore_wait(barrier, len(near) + len(far))
    for i in of_batch(0):
        if parts[i][3]:
            scatter_pair(i)
    for i in of_batch(0):
        if not parts[i][3]:
            scatter_direct(i)
    for load in late:
        load.start()
    for b in range(1, batches):
        means.append(local_partial(b))
        for i in of_batch(b):
            scatter_pair(i)
    for i in of_batch(0):
        if parts[i][3]:
            scatter_sites(i)
    for b in range(batches):
        mean_part[:, b * obs_count:(b + 1) * obs_count] = as_row(means[b])
    for owner, slot in near:
        remote(mean_part, mean_rs.at[slot], mean_sem.at[0], device(owner)).start()
    for b in range(1, batches):
        for i in of_batch(b):
            scatter_sites(i)
    for i in of_batch(0):
        sum_near(i)
    for b in range(1, batches):
        for i in of_batch(b):
            sum_near(i)
    for i in of_batch(0):
        sum_far(i)
    arrived(mean_rs, mean_sem.at[0])
    total = mean_part[...]
    for k in range(len(near)):
        total = total + mean_rs[k]
    mean_zsend[...] = total
    for where, slot in far:
        remote(mean_zsend, mean_z.at[slot], mean_sem.at[1], where).start()
    for b in range(1, batches):
        for i in of_batch(b):
            sum_far(i)
    for i, part in enumerate(parts):
        if part[4]:
            pass_on(i)
    arrived(mean_z, mean_sem.at[1])
    mean_row = mean_zsend[...]
    for k in range(len(far)):
        mean_row = mean_row + mean_z[k]
    for load in early[2 + batches:]:
        load.wait()

    def anomaly(wide):
        return (wide - jnp.mean(wide, axis=1, keepdims=True)).astype(BF16)

    def newton_weights(spread, spread_low, innov, b):
        power = jnp.sum(jnp.sum(spread * spread, axis=0, keepdims=True), axis=1, keepdims=True) / (members - 1)
        centre = (power + jnp.sum(var[b:b + 1, :], axis=1, keepdims=True)) / obs_count
        cov = dot_nt(spread_low, spread_low) / (members - 1) + jnp.where(on_diag, var[b:b + 1, :], 0.0)
        rest = cov - jnp.where(on_diag, centre, 0.0)
        low = rest.astype(BF16)
        bound = jnp.max(jnp.sum(jnp.abs(cov), axis=0, keepdims=True), axis=1, keepdims=True)
        inverse = 1.0 / bound
        shift = 1.0 - centre * inverse
        square = dot(low, low)
        weights = (1.0 + shift) * innov - inverse * dot(low, innov.astype(BF16))
        rest = (inverse * inverse) * square - (2.0 * shift * inverse) * rest
        for step in range(1, NEWTON):
            shift = shift * shift
            low = rest.astype(BF16)
            weights, square = (1.0 + shift) * weights + dot(low, weights.astype(BF16)), dot(low, low)
            rest = square + (2.0 * shift) * rest
        return weights * inverse

    def spread_out(column):
        return jnp.concatenate([column] * (members // column.shape[1]), axis=1)

    state = ens[...].astype(F32)
    anom = anomaly(state)
    targets = []
    for b in range(batches):
        late[b].wait()
        noise = pert[b].astype(F32)
        noise_mean = jnp.mean(noise, axis=1, keepdims=True)
        offset = as_column(obs[b:b + 1, :] - mean_row[:, b * obs_count:(b + 1) * obs_count])
        targets.append((noise - noise_mean, jnp.broadcast_to(noise_mean + offset, (obs_count, 128))))
    priors = [gathered(0)]
    crosses = []
    changes = []
    for b in range(batches):
        spread, middle = priors[b].astype(F32), targets[b][1]
        for k, (cross, earlier) in enumerate(zip(crosses, changes)):
            if k:
                cross = (dot_nt(spread.astype(BF16), history[k]) / (members - 1)).astype(BF16)
            change = dot(cross, earlier)
            spread = spread + change[:, :members]
            middle = middle - change[:, members:]
        spread_low = spread.astype(BF16)
        if b == 0:
            history = [spread_low]
        else:
            history.append(spread_low)
        gain = (dot_nt(anom, spread_low) / (members - 1)).astype(BF16)

        def between():
            priors.append(gathered(b + 1))
            crosses.append((dot_nt(priors[-1], history[0]) / (members - 1)).astype(BF16))

        innov = targets[b][0] - spread
        if b + 1 < batches:
            both = newton_weights(spread, spread_low, jnp.concatenate([innov, middle], axis=1), b)
            changes.append(both.astype(BF16))
            weights = both[:, :members] + spread_out(both[:, members:])
            between()
        else:
            weights = newton_weights(spread, spread_low, innov + spread_out(middle), b)
        low = (state + dot(gain, weights.astype(BF16))).astype(BF16)
        if b + 1 < batches:
            state = low.astype(F32)
            anom = anomaly(state)
    out_ref[...] = low
    pltpu.make_async_remote_copy(
        src_ref=all_sent, dst_ref=all_sent, send_sem=send_sem, recv_sem=send_sem,
        device_id=partner, device_id_type=MESH,
    ).wait_send()


def on_device(ensemble, tiles, tile_live, observed, perturb, obs_var):
    region_count = lax.axis_size("region")
    group_count = lax.axis_size("group")
    batches, obs_count, members = perturb.shape
    planes = PLANES if group_count % PLANES == 0 else 1
    owners = region_count * planes
    chunk_rows = max(16, obs_count // owners)
    chunk_cols = obs_count * members // (owners * chunk_rows)
    sites = owners // CORES
    far = group_count // planes - 1
    crossing = 2 * (sites // planes * (planes - 1))
    parts = [part for b in range(batches) for part in parts_of(b, chunk_cols)]
    rows = 2 * chunk_rows
    sent = sum(
        rows * width * ((sites + sites - 1 if pair else owners - 1) + far + (crossing + region_count - 1 if hop else owners - 1))
        for _, width, pair, hop in parts
    )
    sent += 4 * batches * obs_count * (owners - 1 + far)
    hbm = pl.BlockSpec(memory_space=pl.ANY)
    block = (chunk_rows, chunk_cols)
    dma = pltpu.SemaphoreType.DMA
    return pl.pallas_call(
        functools.partial(kernel, region_count, group_count),
        out_shape=pltpu.VMEM(ensemble.shape, ensemble.dtype),
        in_specs=[hbm] * 6,
        out_specs=pl.BlockSpec(memory_space=pltpu.VMEM),
        scratch_shapes=[
            pltpu.VMEM(ensemble.shape, BF16),
            pltpu.VMEM(tiles.shape, BF16),
            pltpu.VMEM(tile_live.shape, tile_live.dtype),
            pltpu.VMEM(observed.shape, F32),
            pltpu.VMEM(perturb.shape, BF16),
            pltpu.VMEM(obs_var.shape, F32),
            pltpu.VMEM((batches, owners, *block), BF16),
            pltpu.VMEM((owners - 1, *block), BF16),
            pltpu.VMEM((batches, sites, *block), BF16),
            pltpu.VMEM((batches, sites - 1, *block), BF16),
            pltpu.VMEM((batches, sites - 1, *block), BF16),
            pltpu.VMEM((batches, *block), BF16),
            pltpu.VMEM((batches, far, *block), BF16),
            pltpu.VMEM((batches, owners, *block), BF16),
            pltpu.VMEM((1, batches * obs_count), F32),
            pltpu.VMEM((owners - 1, 1, batches * obs_count), F32),
            pltpu.VMEM((1, batches * obs_count), F32),
            pltpu.VMEM((far, 1, batches * obs_count), F32),
            pltpu.VMEM((sent // 512, 128), F32),
            dma((4 + 2 * batches,)),
            dma(()),
            dma((len(parts),)),
            dma((len(parts),)),
            dma((len(parts),)),
            dma((len(parts),)),
            dma((2, 1)),
            dma((2,)),
        ],
        compiler_params=pltpu.CompilerParams(collective_id=0, has_side_effects=True),
    )(ensemble, tiles, tile_live, observed, perturb, obs_var)


def solution(mesh):
    return jax.shard_map(
        on_device,
        mesh=mesh,
        in_specs=(
            P(("region", "group"), None),
            P(None, None, ("region", "group")),
            P(),
            P(),
            P(),
            P(),
        ),
        out_specs=P(("region", "group"), None),
        check_vma=False,
    )
```

```python
import functools

import jax
import jax.numpy as jnp
from jax import lax
from jax.experimental import pallas as pl
from jax.experimental.pallas import tpu as pltpu
from jax.sharding import PartitionSpec as P

NEWTON = 4
CORES = 2
PLANES = 2
F32 = jnp.float32
BF16 = jnp.bfloat16
MESH = pl.DeviceIdType.MESH


def dot(a, b):
    return jnp.dot(a, b, preferred_element_type=F32)


def dot_nt(a, b):
    return lax.dot_general(a, b, (((1,), (1,)), ((), ())), preferred_element_type=F32)


def dot_tn(a, b):
    return lax.dot_general(a, b, (((0,), (0,)), ((), ())), preferred_element_type=F32)


def parts_of(batch, chunk_cols):
    half = chunk_cols // 2
    if batch == 0 and half % 128 == 0:
        return [(0, half, False, True), (half, half, True, False)]
    return [(0, chunk_cols, batch > 0, False)]


def kernel(
    region_count, group_count,
    ens_hbm, tiles_hbm, live_hbm, obs_hbm, pert_hbm, var_hbm,
    out_ref,
    ens, tiles, live, obs, pert, var,
    partial, direct, pair, half_send, half, z_send, z_buf, spread_buf,
    mean_part, mean_rs, mean_zsend, mean_z, all_sent,
    load_sem, send_sem, rs_sem, pair_sem, z_sem, ag_sem, hop_sem, mean_sem,
):
    batches, obs_count, members = pert.shape
    owners, chunk_rows, chunk_cols = partial.shape[1:]
    across = members // chunk_cols
    blocks = owners // across
    planes = owners // region_count
    sites = owners // CORES
    region = lax.axis_index("region")
    group = lax.axis_index("group")
    high, plane = lax.div(group, planes), lax.rem(group, planes)
    mine = plane * region_count + region
    site, core = lax.div(mine, CORES), lax.rem(mine, CORES)

    def others(me, count):
        peers = [k + (me <= k).astype(jnp.int32) for k in range(count - 1)]
        return [(peer, me - (me > peer).astype(jnp.int32)) for peer in peers]

    def device(owner):
        return lax.rem(owner, region_count), high * planes + lax.div(owner, region_count)

    beyond = sites // planes * (planes - 1)
    near = others(mine, owners)
    near_sites = others(site, sites)
    far = [((region, there * planes + plane), slot) for there, slot in others(high, group_count // planes)]
    partner = device(site * CORES + CORES - 1 - core)

    barrier = pltpu.get_barrier_semaphore()
    for owner, _ in near:
        pl.semaphore_signal(barrier, inc=1, device_id=device(owner), device_id_type=MESH)
    for where, _ in far:
        pl.semaphore_signal(barrier, inc=1, device_id=where, device_id_type=MESH)

    sources = [(ens_hbm, ens)]
    sources += [(tiles_hbm.at[b], tiles.at[b]) for b in range(batches)]
    sources += [(live_hbm, live), (obs_hbm, obs), (var_hbm, var), (pert_hbm, pert)]
    loads = [pltpu.make_async_copy(src, dst, load_sem.at[i]) for i, (src, dst) in enumerate(sources)]
    early, late = loads[:4 + batches], loads[4 + batches:]
    for load in early:
        load.start()

    row_at = lax.broadcasted_iota(jnp.int32, (obs_count, obs_count), 0)
    col_at = lax.broadcasted_iota(jnp.int32, (obs_count, obs_count), 1)
    on_diag = row_at == col_at

    def as_row(column):
        return jnp.sum(jnp.where(on_diag, column, 0.0), axis=0, keepdims=True)

    def as_column(row):
        return jnp.sum(jnp.where(on_diag, row, 0.0), axis=1, keepdims=True)

    def remote(src, dst, recv_sem, where):
        return pltpu.make_async_remote_copy(
            src_ref=src, dst_ref=dst, send_sem=send_sem, recv_sem=recv_sem,
            device_id=where, device_id_type=MESH,
        )

    def arrived(ref, recv_sem):
        remote(ref, ref, recv_sem, partner).wait_recv()

    parts = [(b, *part) for b in range(batches) for part in parts_of(b, chunk_cols)]

    paired = [i for i, part in enumerate(parts) if part[3]]
    hops = [i for i, part in enumerate(parts) if part[4]]

    def cols(ref, part):
        return ref.at[..., pl.ds(parts[part][1], parts[part][2])]

    def of_batch(b):
        return [i for i, part in enumerate(parts) if part[0] == b]

    def local_partial(b):
        loads[1 + b].wait()
        value = dot(tiles[b], ens[...]) * live_of[b:b + 1]
        mean = jnp.mean(value, axis=1, keepdims=True)
        value = (value - mean).astype(BF16)
        for a in range(across):
            block = value[:, a * chunk_cols:(a + 1) * chunk_cols]
            partial[b, a * blocks:(a + 1) * blocks] = block.reshape(blocks, chunk_rows, chunk_cols)
        return mean

    def scatter_direct(i):
        b = parts[i][0]
        for owner, slot in near[::-1]:
            remote(cols(partial.at[b, owner], i), cols(direct.at[slot], i), rs_sem.at[i], device(owner)).start()

    def scatter_pair(i):
        b = parts[i][0]
        for k in range(sites):
            src = cols(partial.at[b, k * CORES + CORES - 1 - core], i)
            remote(src, cols(pair.at[b, k], i), pair_sem.at[paired.index(i)], partner).start()

    def scatter_sites(i):
        b = parts[i][0]
        arrived(cols(pair.at[b], i), pair_sem.at[paired.index(i)])
        for k, (there, slot) in list(enumerate(near_sites))[::-1]:
            total = cols(partial.at[b, there * CORES + core], i)[...].astype(F32) + cols(pair.at[b, there], i)[...].astype(F32)
            cols(half_send.at[b, k], i)[...] = total.astype(BF16)
            where = device(there * CORES + core)
            remote(cols(half_send.at[b, k], i), cols(half.at[b, slot], i), rs_sem.at[i], where).start()

    def sum_near(i):
        b = parts[i][0]
        total = cols(partial.at[b, mine], i)[...].astype(F32)
        if parts[i][3]:
            total = total + cols(pair.at[b, site], i)[...].astype(F32)
            arrivals = cols(half.at[b], i)
        else:
            arrivals = cols(direct, i)
        arrived(arrivals, rs_sem.at[i])
        for k in range(arrivals.shape[0]):
            total = total + arrivals[k].astype(F32)
        cols(z_send.at[b], i)[...] = total.astype(BF16)
        for where, slot in far:
            remote(cols(z_send.at[b], i), cols(z_buf.at[b, slot], i), z_sem.at[i], where).start()

    def sum_far(i):
        b = parts[i][0]
        total = cols(z_send.at[b], i)[...].astype(F32)
        arrived(cols(z_buf.at[b], i), z_sem.at[i])
        for k in range(len(far)):
            total = total + cols(z_buf.at[b, k], i)[...].astype(F32)
        ours = cols(spread_buf.at[b, mine], i)
        ours[...] = total.astype(BF16)
        if not parts[i][4]:
            for owner, _ in near:
                remote(ours, ours, ag_sem.at[i], device(owner)).start()
            return
        for there in range(sites // planes * (planes - 1)):
            owner = (there + jnp.where(there >= plane * (sites // planes), sites // planes, 0)) * CORES + core
            remote(ours, ours, hop_sem.at[0, hops.index(i)], device(owner)).start()
        for peer, _ in others(region, region_count):
            remote(ours, ours, ag_sem.at[i], device(plane * region_count + peer)).start()

    def pass_on(i):
        count = sites // planes * (planes - 1)
        arrived(cols(direct.at[pl.ds(0, count)], i), hop_sem.at[0, hops.index(i)])
        for there in range(count):
            owner = (there + jnp.where(there >= plane * (sites // planes), sites // planes, 0)) * CORES + core
            block = cols(spread_buf.at[parts[i][0], owner], i)
            remote(block, block, hop_sem.at[1, hops.index(i)], partner).start()

    def wait_for(i):
        if parts[i][4]:
            arrived(cols(direct.at[pl.ds(0, beyond)], i), hop_sem.at[1, hops.index(i)])
            arrived(cols(direct.at[pl.ds(0, region_count - 1)], i), ag_sem.at[i])
        else:
            arrived(cols(direct, i), ag_sem.at[i])

    def gathered(b, use):
        order = of_batch(b)[::-1]
        if across > 1:
            for i in order:
                wait_for(i)
            whole = [spread_buf[b, a * blocks:(a + 1) * blocks].reshape(obs_count, chunk_cols) for a in range(across)]
            whole = jnp.concatenate(whole, axis=1)
            return whole, use(whole, 0)
        pieces, total = {}, None
        for i in order:
            wait_for(i)
            start = parts[i][1]
            pieces[start] = cols(spread_buf.at[b], i)[...].reshape(obs_count, parts[i][2])
            made = use(pieces[start], start)
            total = made if total is None else [x + y for x, y in zip(total, made)]
        pieces = [pieces[start] for start in sorted(pieces)]
        return (jnp.concatenate(pieces, axis=1) if len(pieces) > 1 else pieces[0]), total

    loads[1 + batches].wait()
    region_at = lax.broadcasted_iota(jnp.int32, live.shape, 1)
    live_of = jnp.sum(jnp.where(region_at == region, live[...].astype(F32), 0.0), axis=1, keepdims=True)
    loads[0].wait()
    means = [local_partial(0)]
    pl.semaphore_wait(barrier, len(near) + len(far))
    for i in of_batch(0):
        if parts[i][3]:
            scatter_pair(i)
    for i in of_batch(0):
        if not parts[i][3]:
            scatter_direct(i)
    for load in late:
        load.start()
    for b in range(1, batches):
        means.append(local_partial(b))
        for i in of_batch(b):
            scatter_pair(i)
    for i in of_batch(0):
        if parts[i][3]:
            scatter_sites(i)
    for b in range(batches):
        mean_part[:, b * obs_count:(b + 1) * obs_count] = as_row(means[b])
    for owner, slot in near:
        remote(mean_part, mean_rs.at[slot], mean_sem.at[0], device(owner)).start()
    for b in range(1, batches):
        for i in of_batch(b):
            scatter_sites(i)
    def anomaly(wide):
        return (wide - jnp.mean(wide, axis=1, keepdims=True)).astype(BF16)

    for load in late:
        load.wait()
    state = ens[...].astype(F32)
    anom = anomaly(state)
    noise = []
    for b in range(batches):
        wide = pert[b].astype(F32)
        middle = jnp.mean(wide, axis=1, keepdims=True)
        noise.append((wide - middle, middle))
    for i in of_batch(0):
        sum_near(i)
    for b in range(1, batches):
        for i in of_batch(b):
            sum_near(i)
    for i in of_batch(0):
        sum_far(i)
    arrived(mean_rs, mean_sem.at[0])
    total = mean_part[...]
    for k in range(len(near)):
        total = total + mean_rs[k]
    mean_zsend[...] = total
    for where, slot in far:
        remote(mean_zsend, mean_z.at[slot], mean_sem.at[1], where).start()
    for b in range(1, batches):
        for i in of_batch(b):
            sum_far(i)
    for i, part in enumerate(parts):
        if part[4]:
            pass_on(i)
    arrived(mean_z, mean_sem.at[1])
    mean_row = mean_zsend[...]
    for k in range(len(far)):
        mean_row = mean_row + mean_z[k]
    for load in early[2 + batches:]:
        load.wait()

    def newton_weights(spread, product, innov, b):
        power = jnp.sum(jnp.sum(spread * spread, axis=0, keepdims=True), axis=1, keepdims=True) / (members - 1)
        centre = (power + jnp.sum(var[b:b + 1, :], axis=1, keepdims=True)) / obs_count
        cov = product / (members - 1) + jnp.where(on_diag, var[b:b + 1, :], 0.0)
        rest = cov - jnp.where(on_diag, centre, 0.0)
        low = rest.astype(BF16)
        bound = jnp.max(jnp.sum(jnp.abs(cov), axis=0, keepdims=True), axis=1, keepdims=True)
        inverse = 1.0 / bound
        shift = 1.0 - centre * inverse
        square = dot(low, low)
        weights = (1.0 + shift) * innov - inverse * dot(low, innov.astype(BF16))
        rest = (inverse * inverse) * square - (2.0 * shift * inverse) * rest
        for step in range(1, NEWTON):
            shift = shift * shift
            low = rest.astype(BF16)
            weights, square = (1.0 + shift) * weights + dot(low, weights.astype(BF16)), dot(low, low)
            rest = square + (2.0 * shift) * rest
        return weights * inverse

    def spread_out(column):
        return jnp.concatenate([column] * (members // column.shape[1]), axis=1)

    targets = []
    for b in range(batches):
        offset = as_column(obs[b:b + 1, :] - mean_row[:, b * obs_count:(b + 1) * obs_count])
        targets.append((noise[b][0], jnp.broadcast_to(noise[b][1] + offset, (obs_count, 128))))
    moves = []
    for b in range(batches):
        def use(piece, start):
            if b:
                return []
            return [dot_nt(piece, piece), dot_nt(anom[:, start:start + piece.shape[1]], piece)]

        prior, made = gathered(b, use)
        spread, middle = prior.astype(F32), targets[b][1]
        for move in moves:
            change = dot(spread.astype(BF16), move)
            spread = spread + change[:, :members]
            middle = middle - change[:, members:]
        spread_low = spread.astype(BF16)
        if b:
            state = (state + dot(*update)).astype(BF16).astype(F32)
            anom = anomaly(state)
            made = [dot_nt(spread_low, spread_low), dot_nt(anom, spread_low)]
        product, gain = made[0], (made[1] / (members - 1)).astype(BF16)
        innov = targets[b][0] - spread
        if b + 1 < batches:
            both = newton_weights(spread, product, jnp.concatenate([innov, middle], axis=1), b)
            moves.append((dot_tn(spread_low, both.astype(BF16)) / (members - 1)).astype(BF16))
            weights = both[:, :members] + spread_out(both[:, members:])
            update = gain, weights.astype(BF16)
        else:
            weights = newton_weights(spread, product, innov + spread_out(middle), b)
            low = (state + dot(gain, weights.astype(BF16))).astype(BF16)
    out_ref[...] = low
    pltpu.make_async_remote_copy(
        src_ref=all_sent, dst_ref=all_sent, send_sem=send_sem, recv_sem=send_sem,
        device_id=partner, device_id_type=MESH,
    ).wait_send()


def on_device(ensemble, tiles, tile_live, observed, perturb, obs_var):
    region_count = lax.axis_size("region")
    group_count = lax.axis_size("group")
    batches, obs_count, members = perturb.shape
    planes = PLANES if group_count % PLANES == 0 else 1
    owners = region_count * planes
    chunk_rows = max(16, obs_count // owners)
    chunk_cols = obs_count * members // (owners * chunk_rows)
    sites = owners // CORES
    far = group_count // planes - 1
    crossing = 2 * (sites // planes * (planes - 1))
    parts = [part for b in range(batches) for part in parts_of(b, chunk_cols)]
    rows = 2 * chunk_rows
    sent = sum(
        rows * width * ((sites + sites - 1 if pair else owners - 1) + far + (crossing + region_count - 1 if hop else owners - 1))
        for _, width, pair, hop in parts
    )
    sent += 4 * batches * obs_count * (owners - 1 + far)
    hbm = pl.BlockSpec(memory_space=pl.ANY)
    block = (chunk_rows, chunk_cols)
    dma = pltpu.SemaphoreType.DMA
    return pl.pallas_call(
        functools.partial(kernel, region_count, group_count),
        out_shape=pltpu.VMEM(ensemble.shape, ensemble.dtype),
        in_specs=[hbm] * 6,
        out_specs=pl.BlockSpec(memory_space=pltpu.VMEM),
        scratch_shapes=[
            pltpu.VMEM(ensemble.shape, BF16),
            pltpu.VMEM(tiles.shape, BF16),
            pltpu.VMEM(tile_live.shape, tile_live.dtype),
            pltpu.VMEM(observed.shape, F32),
            pltpu.VMEM(perturb.shape, BF16),
            pltpu.VMEM(obs_var.shape, F32),
            pltpu.VMEM((batches, owners, *block), BF16),
            pltpu.VMEM((owners - 1, *block), BF16),
            pltpu.VMEM((batches, sites, *block), BF16),
            pltpu.VMEM((batches, sites - 1, *block), BF16),
            pltpu.VMEM((batches, sites - 1, *block), BF16),
            pltpu.VMEM((batches, *block), BF16),
            pltpu.VMEM((batches, far, *block), BF16),
            pltpu.VMEM((batches, owners, *block), BF16),
            pltpu.VMEM((1, batches * obs_count), F32),
            pltpu.VMEM((owners - 1, 1, batches * obs_count), F32),
            pltpu.VMEM((1, batches * obs_count), F32),
            pltpu.VMEM((far, 1, batches * obs_count), F32),
            pltpu.VMEM((sent // 512, 128), F32),
            dma((5 + batches,)),
            dma(()),
            dma((len(parts),)),
            dma((max(1, sum(part[2] for part in parts)),)),
            dma((len(parts),)),
            dma((len(parts),)),
            dma((2, max(1, sum(part[3] for part in parts)))),
            dma((2,)),
        ],
        compiler_params=pltpu.CompilerParams(collective_id=0, has_side_effects=True),
    )(ensemble, tiles, tile_live, observed, perturb, obs_var)


def solution(mesh):
    return jax.shard_map(
        on_device,
        mesh=mesh,
        in_specs=(
            P(("region", "group"), None),
            P(None, None, ("region", "group")),
            P(),
            P(),
            P(),
            P(),
        ),
        out_specs=P(("region", "group"), None),
        check_vma=False,
    )
```

```python
import functools

import jax
import jax.numpy as jnp
from jax import lax
from jax.experimental import pallas as pl
from jax.experimental.pallas import tpu as pltpu
from jax.sharding import PartitionSpec as P

NEWTON = 4
CORES = 2
PLANES = 2
F32 = jnp.float32
BF16 = jnp.bfloat16
MESH = pl.DeviceIdType.MESH


def dot(a, b):
    return jnp.dot(a, b, preferred_element_type=F32)


def dot_nt(a, b):
    return lax.dot_general(a, b, (((1,), (1,)), ((), ())), preferred_element_type=F32)


def dot_tn(a, b):
    return lax.dot_general(a, b, (((0,), (0,)), ((), ())), preferred_element_type=F32)


def parts_of(batch, chunk_cols):
    half = chunk_cols // 2
    if batch == 0 and half % 128 == 0:
        return [(0, half, False, True), (half, half, True, False)]
    return [(0, chunk_cols, batch > 0, False)]


def kernel(
    region_count, group_count,
    ens_hbm, tiles_hbm, live_hbm, obs_hbm, pert_hbm, var_hbm,
    out_ref,
    ens, tiles, live, obs, pert, var,
    partial, direct, pair, half_send, half, z_send, z_buf, spread_buf,
    mean_part, mean_rs, mean_zsend, mean_z, all_sent,
    load_sem, send_sem, rs_sem, pair_sem, z_sem, ag_sem, hop_sem, mean_sem,
):
    batches, obs_count, members = pert.shape
    owners, chunk_rows, chunk_cols = partial.shape[1:]
    across = members // chunk_cols
    blocks = owners // across
    planes = owners // region_count
    sites = owners // CORES
    region = lax.axis_index("region")
    group = lax.axis_index("group")
    high, plane = lax.div(group, planes), lax.rem(group, planes)
    mine = plane * region_count + region
    site, core = lax.div(mine, CORES), lax.rem(mine, CORES)

    def others(me, count):
        peers = [k + (me <= k).astype(jnp.int32) for k in range(count - 1)]
        return [(peer, me - (me > peer).astype(jnp.int32)) for peer in peers]

    def device(owner):
        return lax.rem(owner, region_count), high * planes + lax.div(owner, region_count)

    near = others(mine, owners)
    near_sites = others(site, sites)
    far = [((region, there * planes + plane), slot) for there, slot in others(high, group_count // planes)]
    partner = device(site * CORES + CORES - 1 - core)

    barrier = pltpu.get_barrier_semaphore()
    for owner, _ in near:
        pl.semaphore_signal(barrier, inc=1, device_id=device(owner), device_id_type=MESH)
    for where, _ in far:
        pl.semaphore_signal(barrier, inc=1, device_id=where, device_id_type=MESH)

    sources = [(ens_hbm, ens)]
    sources += [(tiles_hbm.at[b], tiles.at[b]) for b in range(batches)]
    sources += [(live_hbm, live), (obs_hbm, obs), (var_hbm, var), (pert_hbm, pert)]
    loads = [pltpu.make_async_copy(src, dst, load_sem.at[i]) for i, (src, dst) in enumerate(sources)]
    early, late = loads[:4 + batches], loads[4 + batches:]
    for load in early:
        load.start()

    row_at = lax.broadcasted_iota(jnp.int32, (obs_count, obs_count), 0)
    col_at = lax.broadcasted_iota(jnp.int32, (obs_count, obs_count), 1)
    on_diag = row_at == col_at

    def as_row(column):
        return jnp.sum(jnp.where(on_diag, column, 0.0), axis=0, keepdims=True)

    def as_column(row):
        return jnp.sum(jnp.where(on_diag, row, 0.0), axis=1, keepdims=True)

    def remote(src, dst, recv_sem, where):
        return pltpu.make_async_remote_copy(
            src_ref=src, dst_ref=dst, send_sem=send_sem, recv_sem=recv_sem,
            device_id=where, device_id_type=MESH,
        )

    def arrived(ref, recv_sem):
        remote(ref, ref, recv_sem, partner).wait_recv()

    parts = [(b, *part) for b in range(batches) for part in parts_of(b, chunk_cols)]

    paired = [i for i, part in enumerate(parts) if part[3]]
    hops = [i for i, part in enumerate(parts) if part[4]]

    def cols(ref, part):
        return ref.at[..., pl.ds(parts[part][1], parts[part][2])]

    def of_batch(b):
        return [i for i, part in enumerate(parts) if part[0] == b]

    def local_partial(b):
        loads[1 + b].wait()
        value = dot(tiles[b], ens[...]) * live_of[b:b + 1]
        mean = jnp.mean(value, axis=1, keepdims=True)
        value = (value - mean).astype(BF16)
        for a in range(across):
            block = value[:, a * chunk_cols:(a + 1) * chunk_cols]
            partial[b, a * blocks:(a + 1) * blocks] = block.reshape(blocks, chunk_rows, chunk_cols)
        return mean

    def scatter_direct(i):
        b = parts[i][0]
        for owner, slot in near[::-1]:
            remote(cols(partial.at[b, owner], i), cols(direct.at[slot], i), rs_sem.at[i], device(owner)).start()

    def scatter_pair(i):
        b = parts[i][0]
        for k in range(sites):
            src = cols(partial.at[b, k * CORES + CORES - 1 - core], i)
            remote(src, cols(pair.at[b, k], i), pair_sem.at[paired.index(i)], partner).start()

    def scatter_sites(i):
        b = parts[i][0]
        arrived(cols(pair.at[b], i), pair_sem.at[paired.index(i)])
        for k, (there, slot) in list(enumerate(near_sites))[::-1]:
            total = cols(partial.at[b, there * CORES + core], i)[...].astype(F32) + cols(pair.at[b, there], i)[...].astype(F32)
            cols(half_send.at[b, k], i)[...] = total.astype(BF16)
            where = device(there * CORES + core)
            remote(cols(half_send.at[b, k], i), cols(half.at[b, slot], i), rs_sem.at[i], where).start()

    def sum_near(i):
        b = parts[i][0]
        total = cols(partial.at[b, mine], i)[...].astype(F32)
        if parts[i][3]:
            total = total + cols(pair.at[b, site], i)[...].astype(F32)
            arrivals = cols(half.at[b], i)
        else:
            arrivals = cols(direct, i)
        arrived(arrivals, rs_sem.at[i])
        for k in range(arrivals.shape[0]):
            total = total + arrivals[k].astype(F32)
        cols(z_send.at[b], i)[...] = total.astype(BF16)
        for where, slot in far:
            remote(cols(z_send.at[b], i), cols(z_buf.at[b, slot], i), z_sem.at[i], where).start()

    def sum_far(i):
        b = parts[i][0]
        total = cols(z_send.at[b], i)[...].astype(F32)
        arrived(cols(z_buf.at[b], i), z_sem.at[i])
        for k in range(len(far)):
            total = total + cols(z_buf.at[b, k], i)[...].astype(F32)
        ours = cols(spread_buf.at[b, mine], i)
        ours[...] = total.astype(BF16)
        if not parts[i][4]:
            for owner, _ in near:
                remote(ours, ours, ag_sem.at[i], device(owner)).start()
            return
        for there, _ in near_sites:
            remote(ours, ours, hop_sem.at[0, hops.index(i)], device(there * CORES + core)).start()
        remote(ours, ours, ag_sem.at[i], partner).start()

    def pass_on(i):
        arrived(cols(direct.at[pl.ds(0, sites - 1)], i), hop_sem.at[0, hops.index(i)])
        for there, _ in near_sites:
            block = cols(spread_buf.at[parts[i][0], there * CORES + core], i)
            remote(block, block, hop_sem.at[1, hops.index(i)], partner).start()

    def wait_for(i):
        if parts[i][4]:
            arrived(cols(direct.at[pl.ds(0, sites - 1)], i), hop_sem.at[1, hops.index(i)])
            arrived(cols(direct.at[0], i), ag_sem.at[i])
        else:
            arrived(cols(direct, i), ag_sem.at[i])

    def gathered(b, use):
        order = of_batch(b)[::-1]
        if across > 1:
            for i in order:
                wait_for(i)
            whole = [spread_buf[b, a * blocks:(a + 1) * blocks].reshape(obs_count, chunk_cols) for a in range(across)]
            whole = jnp.concatenate(whole, axis=1)
            return whole, use(whole, 0)
        pieces, total = {}, None
        for i in order:
            wait_for(i)
            start = parts[i][1]
            pieces[start] = cols(spread_buf.at[b], i)[...].reshape(obs_count, parts[i][2])
            made = use(pieces[start], start)
            total = made if total is None else [x + y for x, y in zip(total, made)]
        pieces = [pieces[start] for start in sorted(pieces)]
        return (jnp.concatenate(pieces, axis=1) if len(pieces) > 1 else pieces[0]), total

    loads[1 + batches].wait()
    region_at = lax.broadcasted_iota(jnp.int32, live.shape, 1)
    live_of = jnp.sum(jnp.where(region_at == region, live[...].astype(F32), 0.0), axis=1, keepdims=True)
    loads[0].wait()
    means = [local_partial(0)]
    pl.semaphore_wait(barrier, len(near) + len(far))
    for i in of_batch(0):
        if parts[i][3]:
            scatter_pair(i)
    for i in of_batch(0):
        if not parts[i][3]:
            scatter_direct(i)
    for load in late:
        load.start()
    for b in range(1, batches):
        means.append(local_partial(b))
        for i in of_batch(b):
            scatter_pair(i)
    for i in of_batch(0):
        if parts[i][3]:
            scatter_sites(i)
    for b in range(batches):
        mean_part[:, b * obs_count:(b + 1) * obs_count] = as_row(means[b])
    for owner, slot in near:
        remote(mean_part, mean_rs.at[slot], mean_sem.at[0], device(owner)).start()
    for b in range(1, batches):
        for i in of_batch(b):
            scatter_sites(i)
    def anomaly(wide):
        return (wide - jnp.mean(wide, axis=1, keepdims=True)).astype(BF16)

    for load in late:
        load.wait()
    state = ens[...].astype(F32)
    anom = anomaly(state)
    noise = []
    for b in range(batches):
        wide = pert[b].astype(F32)
        middle = jnp.mean(wide, axis=1, keepdims=True)
        noise.append((wide - middle, middle))
    for i in of_batch(0):
        sum_near(i)
    for b in range(1, batches):
        for i in of_batch(b):
            sum_near(i)
    for i in of_batch(0):
        sum_far(i)
    arrived(mean_rs, mean_sem.at[0])
    total = mean_part[...]
    for k in range(len(near)):
        total = total + mean_rs[k]
    mean_zsend[...] = total
    for where, slot in far:
        remote(mean_zsend, mean_z.at[slot], mean_sem.at[1], where).start()
    for b in range(1, batches):
        for i in of_batch(b):
            sum_far(i)
    for i, part in enumerate(parts):
        if part[4]:
            pass_on(i)
    arrived(mean_z, mean_sem.at[1])
    mean_row = mean_zsend[...]
    for k in range(len(far)):
        mean_row = mean_row + mean_z[k]
    for load in early[2 + batches:]:
        load.wait()

    def newton_weights(spread, product, innov, b):
        power = jnp.sum(jnp.sum(spread * spread, axis=0, keepdims=True), axis=1, keepdims=True) / (members - 1)
        centre = (power + jnp.sum(var[b:b + 1, :], axis=1, keepdims=True)) / obs_count
        cov = product / (members - 1) + jnp.where(on_diag, var[b:b + 1, :], 0.0)
        rest = cov - jnp.where(on_diag, centre, 0.0)
        low = rest.astype(BF16)
        bound = jnp.max(jnp.sum(jnp.abs(cov), axis=0, keepdims=True), axis=1, keepdims=True)
        inverse = 1.0 / bound
        shift = 1.0 - centre * inverse
        square = dot(low, low)
        weights = (1.0 + shift) * innov - inverse * dot(low, innov.astype(BF16))
        rest = (inverse * inverse) * square - (2.0 * shift * inverse) * rest
        for step in range(1, NEWTON):
            shift = shift * shift
            low = rest.astype(BF16)
            weights, square = (1.0 + shift) * weights + dot(low, weights.astype(BF16)), dot(low, low)
            rest = square + (2.0 * shift) * rest
        return weights * inverse

    def spread_out(column):
        return jnp.concatenate([column] * (members // column.shape[1]), axis=1)

    targets = []
    for b in range(batches):
        offset = as_column(obs[b:b + 1, :] - mean_row[:, b * obs_count:(b + 1) * obs_count])
        targets.append((noise[b][0], jnp.broadcast_to(noise[b][1] + offset, (obs_count, 128))))
    moves = []
    for b in range(batches):
        def use(piece, start):
            if b:
                return []
            return [dot_nt(piece, piece), dot_nt(anom[:, start:start + piece.shape[1]], piece)]

        prior, made = gathered(b, use)
        spread, middle = prior.astype(F32), targets[b][1]
        for move in moves:
            change = dot(spread.astype(BF16), move)
            spread = spread + change[:, :members]
            middle = middle - change[:, members:]
        spread_low = spread.astype(BF16)
        if b:
            state = (state + dot(*update)).astype(BF16).astype(F32)
            anom = anomaly(state)
            made = [dot_nt(spread_low, spread_low), dot_nt(anom, spread_low)]
        product, gain = made[0], (made[1] / (members - 1)).astype(BF16)
        innov = targets[b][0] - spread
        if b + 1 < batches:
            both = newton_weights(spread, product, jnp.concatenate([innov, middle], axis=1), b)
            moves.append((dot_tn(spread_low, both.astype(BF16)) / (members - 1)).astype(BF16))
            weights = both[:, :members] + spread_out(both[:, members:])
            update = gain, weights.astype(BF16)
        else:
            weights = newton_weights(spread, product, innov + spread_out(middle), b)
            low = (state + dot(gain, weights.astype(BF16))).astype(BF16)
    out_ref[...] = low
    pltpu.make_async_remote_copy(
        src_ref=all_sent, dst_ref=all_sent, send_sem=send_sem, recv_sem=send_sem,
        device_id=partner, device_id_type=MESH,
    ).wait_send()


def on_device(ensemble, tiles, tile_live, observed, perturb, obs_var):
    region_count = lax.axis_size("region")
    group_count = lax.axis_size("group")
    batches, obs_count, members = perturb.shape
    planes = PLANES if group_count % PLANES == 0 else 1
    owners = region_count * planes
    chunk_rows = max(16, obs_count // owners)
    chunk_cols = obs_count * members // (owners * chunk_rows)
    sites = owners // CORES
    far = group_count // planes - 1
    parts = [part for b in range(batches) for part in parts_of(b, chunk_cols)]
    rows = 2 * chunk_rows
    sent = sum(
        rows * width * ((sites + sites - 1 if pair else owners - 1) + far + (2 * (sites - 1) + 1 if hop else owners - 1))
        for _, width, pair, hop in parts
    )
    sent += 4 * batches * obs_count * (owners - 1 + far)
    hbm = pl.BlockSpec(memory_space=pl.ANY)
    block = (chunk_rows, chunk_cols)
    dma = pltpu.SemaphoreType.DMA
    return pl.pallas_call(
        functools.partial(kernel, region_count, group_count),
        out_shape=pltpu.VMEM(ensemble.shape, ensemble.dtype),
        in_specs=[hbm] * 6,
        out_specs=pl.BlockSpec(memory_space=pltpu.VMEM),
        scratch_shapes=[
            pltpu.VMEM(ensemble.shape, BF16),
            pltpu.VMEM(tiles.shape, BF16),
            pltpu.VMEM(tile_live.shape, tile_live.dtype),
            pltpu.VMEM(observed.shape, F32),
            pltpu.VMEM(perturb.shape, BF16),
            pltpu.VMEM(obs_var.shape, F32),
            pltpu.VMEM((batches, owners, *block), BF16),
            pltpu.VMEM((owners - 1, *block), BF16),
            pltpu.VMEM((batches, sites, *block), BF16),
            pltpu.VMEM((batches, sites - 1, *block), BF16),
            pltpu.VMEM((batches, sites - 1, *block), BF16),
            pltpu.VMEM((batches, *block), BF16),
            pltpu.VMEM((batches, far, *block), BF16),
            pltpu.VMEM((batches, owners, *block), BF16),
            pltpu.VMEM((1, batches * obs_count), F32),
            pltpu.VMEM((owners - 1, 1, batches * obs_count), F32),
            pltpu.VMEM((1, batches * obs_count), F32),
            pltpu.VMEM((far, 1, batches * obs_count), F32),
            pltpu.VMEM((sent // 512, 128), F32),
            dma((5 + batches,)),
            dma(()),
            dma((len(parts),)),
            dma((max(1, sum(part[2] for part in parts)),)),
            dma((len(parts),)),
            dma((len(parts),)),
            dma((2, max(1, sum(part[3] for part in parts)))),
            dma((2,)),
        ],
        compiler_params=pltpu.CompilerParams(collective_id=0, has_side_effects=True),
    )(ensemble, tiles, tile_live, observed, perturb, obs_var)


def solution(mesh):
    return jax.shard_map(
        on_device,
        mesh=mesh,
        in_specs=(
            P(("region", "group"), None),
            P(None, None, ("region", "group")),
            P(),
            P(),
            P(),
            P(),
        ),
        out_specs=P(("region", "group"), None),
        check_vma=False,
    )
```

```python
import functools

import jax
import jax.numpy as jnp
from jax import lax
from jax.experimental import pallas as pl
from jax.experimental.pallas import tpu as pltpu
from jax.sharding import PartitionSpec as P

NEWTON = 4
CORES = 2
PLANES = 2
F32 = jnp.float32
BF16 = jnp.bfloat16
MESH = pl.DeviceIdType.MESH


def dot(a, b):
    return jnp.dot(a, b, preferred_element_type=F32)


def dot_nt(a, b):
    return lax.dot_general(a, b, (((1,), (1,)), ((), ())), preferred_element_type=F32)


def dot_tn(a, b):
    return lax.dot_general(a, b, (((0,), (0,)), ((), ())), preferred_element_type=F32)


def parts_of(batch, chunk_cols):
    half = chunk_cols // 2
    if batch == 0 and half % 128 == 0:
        return [(0, half, False, True), (half, half, True, False)]
    return [(0, chunk_cols, batch > 0, False)]


def kernel(
    region_count, group_count,
    ens_hbm, tiles_hbm, live_hbm, obs_hbm, pert_hbm, var_hbm,
    out_ref,
    ens, tiles, live, obs, pert, var,
    partial, direct, pair, half_send, half, z_send, z_buf, spread_buf,
    mean_part, mean_rs, mean_zsend, mean_z, all_sent,
    load_sem, send_sem, rs_sem, pair_sem, z_sem, ag_sem, hop_sem, mean_sem,
):
    batches, obs_count, members = pert.shape
    owners, chunk_rows, chunk_cols = partial.shape[1:]
    across = members // chunk_cols
    blocks = owners // across
    planes = owners // region_count
    sites = owners // CORES
    region = lax.axis_index("region")
    group = lax.axis_index("group")
    high, plane = lax.div(group, planes), lax.rem(group, planes)
    mine = plane * region_count + region
    site, core = lax.div(mine, CORES), lax.rem(mine, CORES)

    def others(me, count):
        peers = [k + (me <= k).astype(jnp.int32) for k in range(count - 1)]
        return [(peer, me - (me > peer).astype(jnp.int32)) for peer in peers]

    def device(owner):
        return lax.rem(owner, region_count), high * planes + lax.div(owner, region_count)

    near = others(mine, owners)
    near_sites = others(site, sites)
    far = [((region, there * planes + plane), slot) for there, slot in others(high, group_count // planes)]
    partner = device(site * CORES + CORES - 1 - core)

    barrier = pltpu.get_barrier_semaphore()
    for owner, _ in near:
        pl.semaphore_signal(barrier, inc=1, device_id=device(owner), device_id_type=MESH)
    for where, _ in far:
        pl.semaphore_signal(barrier, inc=1, device_id=where, device_id_type=MESH)

    sources = [(ens_hbm, ens)]
    sources += [(tiles_hbm.at[b], tiles.at[b]) for b in range(batches)]
    sources += [(live_hbm, live), (obs_hbm, obs), (var_hbm, var), (pert_hbm, pert)]
    loads = [pltpu.make_async_copy(src, dst, load_sem.at[i]) for i, (src, dst) in enumerate(sources)]
    early, late = loads[:4 + batches], loads[4 + batches:]
    for load in early:
        load.start()

    row_at = lax.broadcasted_iota(jnp.int32, (obs_count, obs_count), 0)
    col_at = lax.broadcasted_iota(jnp.int32, (obs_count, obs_count), 1)
    on_diag = row_at == col_at

    def as_row(column):
        return jnp.sum(jnp.where(on_diag, column, 0.0), axis=0, keepdims=True)

    def as_column(row):
        return jnp.sum(jnp.where(on_diag, row, 0.0), axis=1, keepdims=True)

    def remote(src, dst, recv_sem, where):
        return pltpu.make_async_remote_copy(
            src_ref=src, dst_ref=dst, send_sem=send_sem, recv_sem=recv_sem,
            device_id=where, device_id_type=MESH,
        )

    def arrived(ref, recv_sem):
        remote(ref, ref, recv_sem, partner).wait_recv()

    parts = [(b, *part) for b in range(batches) for part in parts_of(b, chunk_cols)]

    paired = [i for i, part in enumerate(parts) if part[3]]
    hops = [i for i, part in enumerate(parts) if part[4]]

    def cols(ref, part):
        return ref.at[..., pl.ds(parts[part][1], parts[part][2])]

    def of_batch(b):
        return [i for i, part in enumerate(parts) if part[0] == b]

    def local_partial(b):
        loads[1 + b].wait()
        value = dot(tiles[b], ens[...]) * live_of[b:b + 1]
        mean = jnp.mean(value, axis=1, keepdims=True)
        value = (value - mean).astype(BF16)
        for a in range(across):
            block = value[:, a * chunk_cols:(a + 1) * chunk_cols]
            partial[b, a * blocks:(a + 1) * blocks] = block.reshape(blocks, chunk_rows, chunk_cols)
        return mean

    def scatter_direct(i):
        b = parts[i][0]
        for owner, slot in near[::-1]:
            remote(cols(partial.at[b, owner], i), cols(direct.at[slot], i), rs_sem.at[i], device(owner)).start()

    def scatter_pair(i):
        b = parts[i][0]
        for k in range(sites):
            src = cols(partial.at[b, k * CORES + CORES - 1 - core], i)
            remote(src, cols(pair.at[b, k], i), pair_sem.at[paired.index(i)], partner).start()

    def scatter_sites(i):
        b = parts[i][0]
        arrived(cols(pair.at[b], i), pair_sem.at[paired.index(i)])
        for k, (there, slot) in list(enumerate(near_sites))[::-1]:
            total = cols(partial.at[b, there * CORES + core], i)[...].astype(F32) + cols(pair.at[b, there], i)[...].astype(F32)
            cols(half_send.at[b, k], i)[...] = total.astype(BF16)
            where = device(there * CORES + core)
            remote(cols(half_send.at[b, k], i), cols(half.at[b, slot], i), rs_sem.at[i], where).start()

    def sum_near(i):
        b = parts[i][0]
        total = cols(partial.at[b, mine], i)[...].astype(F32)
        if parts[i][3]:
            total = total + cols(pair.at[b, site], i)[...].astype(F32)
            arrivals = cols(half.at[b], i)
        else:
            arrivals = cols(direct, i)
        arrived(arrivals, rs_sem.at[i])
        for k in range(arrivals.shape[0]):
            total = total + arrivals[k].astype(F32)
        cols(z_send.at[b], i)[...] = total.astype(BF16)
        for where, slot in far:
            remote(cols(z_send.at[b], i), cols(z_buf.at[b, slot], i), z_sem.at[i], where).start()

    def sum_far(i):
        b = parts[i][0]
        total = cols(z_send.at[b], i)[...].astype(F32)
        arrived(cols(z_buf.at[b], i), z_sem.at[i])
        for k in range(len(far)):
            total = total + cols(z_buf.at[b, k], i)[...].astype(F32)
        ours = cols(spread_buf.at[b, mine], i)
        ours[...] = total.astype(BF16)
        if not parts[i][4]:
            for owner, _ in near:
                remote(ours, ours, ag_sem.at[i], device(owner)).start()
            return
        for there, _ in near_sites:
            remote(ours, ours, hop_sem.at[0, hops.index(i)], device(there * CORES + core)).start()
        remote(ours, ours, ag_sem.at[i], partner).start()

    def pass_on(i):
        arrived(cols(direct.at[pl.ds(0, sites - 1)], i), hop_sem.at[0, hops.index(i)])
        for there, _ in near_sites:
            block = cols(spread_buf.at[parts[i][0], there * CORES + core], i)
            remote(block, block, hop_sem.at[1, hops.index(i)], partner).start()

    def wait_for(i):
        if parts[i][4]:
            arrived(cols(direct.at[pl.ds(0, sites - 1)], i), hop_sem.at[1, hops.index(i)])
            arrived(cols(direct.at[0], i), ag_sem.at[i])
        else:
            arrived(cols(direct, i), ag_sem.at[i])

    def gathered(b, use):
        order = of_batch(b)[::-1]
        if across > 1:
            for i in order:
                wait_for(i)
            whole = [spread_buf[b, a * blocks:(a + 1) * blocks].reshape(obs_count, chunk_cols) for a in range(across)]
            whole = jnp.concatenate(whole, axis=1)
            return whole, use(whole, 0)
        pieces, total = {}, None
        for i in order:
            wait_for(i)
            start = parts[i][1]
            pieces[start] = cols(spread_buf.at[b], i)[...].reshape(obs_count, parts[i][2])
            made = use(pieces[start], start)
            total = made if total is None else [x + y for x, y in zip(total, made)]
        pieces = [pieces[start] for start in sorted(pieces)]
        return (jnp.concatenate(pieces, axis=1) if len(pieces) > 1 else pieces[0]), total

    loads[1 + batches].wait()
    region_at = lax.broadcasted_iota(jnp.int32, live.shape, 1)
    live_of = jnp.sum(jnp.where(region_at == region, live[...].astype(F32), 0.0), axis=1, keepdims=True)
    loads[0].wait()
    means = [local_partial(0)]
    pl.semaphore_wait(barrier, len(near) + len(far))
    for i in of_batch(0):
        if not parts[i][3]:
            scatter_direct(i)
    for i in of_batch(0):
        if parts[i][3]:
            scatter_pair(i)
    for load in late:
        load.start()
    for b in range(1, batches):
        means.append(local_partial(b))
        for i in of_batch(b):
            scatter_pair(i)
    for i in of_batch(0):
        if parts[i][3]:
            scatter_sites(i)
    for b in range(batches):
        mean_part[:, b * obs_count:(b + 1) * obs_count] = as_row(means[b])
    for owner, slot in near:
        remote(mean_part, mean_rs.at[slot], mean_sem.at[0], device(owner)).start()
    for b in range(1, batches):
        for i in of_batch(b):
            scatter_sites(i)
    def anomaly(wide):
        return (wide - jnp.mean(wide, axis=1, keepdims=True)).astype(BF16)

    for load in late:
        load.wait()
    state = ens[...].astype(F32)
    anom = anomaly(state)
    noise = []
    for b in range(batches):
        wide = pert[b].astype(F32)
        middle = jnp.mean(wide, axis=1, keepdims=True)
        noise.append((wide - middle, middle))
    for i in of_batch(0):
        sum_near(i)
    for b in range(1, batches):
        for i in of_batch(b):
            sum_near(i)
    for i in of_batch(0):
        sum_far(i)
    arrived(mean_rs, mean_sem.at[0])
    total = mean_part[...]
    for k in range(len(near)):
        total = total + mean_rs[k]
    mean_zsend[...] = total
    for where, slot in far:
        remote(mean_zsend, mean_z.at[slot], mean_sem.at[1], where).start()
    for b in range(1, batches):
        for i in of_batch(b):
            sum_far(i)
    for i, part in enumerate(parts):
        if part[4]:
            pass_on(i)
    arrived(mean_z, mean_sem.at[1])
    mean_row = mean_zsend[...]
    for k in range(len(far)):
        mean_row = mean_row + mean_z[k]
    for load in early[2 + batches:]:
        load.wait()

    def newton_weights(spread, product, innov, b):
        power = jnp.sum(jnp.sum(spread * spread, axis=0, keepdims=True), axis=1, keepdims=True) / (members - 1)
        centre = (power + jnp.sum(var[b:b + 1, :], axis=1, keepdims=True)) / obs_count
        cov = product / (members - 1) + jnp.where(on_diag, var[b:b + 1, :], 0.0)
        rest = cov - jnp.where(on_diag, centre, 0.0)
        low = rest.astype(BF16)
        bound = jnp.max(jnp.sum(jnp.abs(cov), axis=0, keepdims=True), axis=1, keepdims=True)
        inverse = 1.0 / bound
        shift = 1.0 - centre * inverse
        square = dot(low, low)
        weights = (1.0 + shift) * innov - inverse * dot(low, innov.astype(BF16))
        rest = (inverse * inverse) * square - (2.0 * shift * inverse) * rest
        for step in range(1, NEWTON):
            shift = shift * shift
            low = rest.astype(BF16)
            weights, square = (1.0 + shift) * weights + dot(low, weights.astype(BF16)), dot(low, low)
            rest = square + (2.0 * shift) * rest
        return weights * inverse

    def spread_out(column):
        return jnp.concatenate([column] * (members // column.shape[1]), axis=1)

    targets = []
    for b in range(batches):
        offset = as_column(obs[b:b + 1, :] - mean_row[:, b * obs_count:(b + 1) * obs_count])
        targets.append((noise[b][0], jnp.broadcast_to(noise[b][1] + offset, (obs_count, 128))))
    moves = []
    for b in range(batches):
        def use(piece, start):
            if b:
                return []
            return [dot_nt(piece, piece), dot_nt(anom[:, start:start + piece.shape[1]], piece)]

        prior, made = gathered(b, use)
        spread, middle = prior.astype(F32), targets[b][1]
        for move in moves:
            change = dot(spread.astype(BF16), move)
            spread = spread + change[:, :members]
            middle = middle - change[:, members:]
        spread_low = spread.astype(BF16)
        if b:
            state = (state + dot(*update)).astype(BF16).astype(F32)
            anom = anomaly(state)
            made = [dot_nt(spread_low, spread_low), dot_nt(anom, spread_low)]
        product, gain = made[0], (made[1] / (members - 1)).astype(BF16)
        innov = targets[b][0] - spread
        if b + 1 < batches:
            both = newton_weights(spread, product, jnp.concatenate([innov, middle], axis=1), b)
            moves.append((dot_tn(spread_low, both.astype(BF16)) / (members - 1)).astype(BF16))
            weights = both[:, :members] + spread_out(both[:, members:])
            update = gain, weights.astype(BF16)
        else:
            weights = newton_weights(spread, product, innov + spread_out(middle), b)
            low = (state + dot(gain, weights.astype(BF16))).astype(BF16)
    out_ref[...] = low
    pltpu.make_async_remote_copy(
        src_ref=all_sent, dst_ref=all_sent, send_sem=send_sem, recv_sem=send_sem,
        device_id=partner, device_id_type=MESH,
    ).wait_send()


def on_device(ensemble, tiles, tile_live, observed, perturb, obs_var):
    region_count = lax.axis_size("region")
    group_count = lax.axis_size("group")
    batches, obs_count, members = perturb.shape
    planes = PLANES if group_count % PLANES == 0 else 1
    owners = region_count * planes
    chunk_rows = max(16, obs_count // owners)
    chunk_cols = obs_count * members // (owners * chunk_rows)
    sites = owners // CORES
    far = group_count // planes - 1
    parts = [part for b in range(batches) for part in parts_of(b, chunk_cols)]
    rows = 2 * chunk_rows
    sent = sum(
        rows * width * ((sites + sites - 1 if pair else owners - 1) + far + (2 * (sites - 1) + 1 if hop else owners - 1))
        for _, width, pair, hop in parts
    )
    sent += 4 * batches * obs_count * (owners - 1 + far)
    hbm = pl.BlockSpec(memory_space=pl.ANY)
    block = (chunk_rows, chunk_cols)
    dma = pltpu.SemaphoreType.DMA
    return pl.pallas_call(
        functools.partial(kernel, region_count, group_count),
        out_shape=pltpu.VMEM(ensemble.shape, ensemble.dtype),
        in_specs=[hbm] * 6,
        out_specs=pl.BlockSpec(memory_space=pltpu.VMEM),
        scratch_shapes=[
            pltpu.VMEM(ensemble.shape, BF16),
            pltpu.VMEM(tiles.shape, BF16),
            pltpu.VMEM(tile_live.shape, tile_live.dtype),
            pltpu.VMEM(observed.shape, F32),
            pltpu.VMEM(perturb.shape, BF16),
            pltpu.VMEM(obs_var.shape, F32),
            pltpu.VMEM((batches, owners, *block), BF16),
            pltpu.VMEM((owners - 1, *block), BF16),
            pltpu.VMEM((batches, sites, *block), BF16),
            pltpu.VMEM((batches, sites - 1, *block), BF16),
            pltpu.VMEM((batches, sites - 1, *block), BF16),
            pltpu.VMEM((batches, *block), BF16),
            pltpu.VMEM((batches, far, *block), BF16),
            pltpu.VMEM((batches, owners, *block), BF16),
            pltpu.VMEM((1, batches * obs_count), F32),
            pltpu.VMEM((owners - 1, 1, batches * obs_count), F32),
            pltpu.VMEM((1, batches * obs_count), F32),
            pltpu.VMEM((far, 1, batches * obs_count), F32),
            pltpu.VMEM((sent // 512, 128), F32),
            dma((5 + batches,)),
            dma(()),
            dma((len(parts),)),
            dma((max(1, sum(part[2] for part in parts)),)),
            dma((len(parts),)),
            dma((len(parts),)),
            dma((2, max(1, sum(part[3] for part in parts)))),
            dma((2,)),
        ],
        compiler_params=pltpu.CompilerParams(collective_id=0, has_side_effects=True),
    )(ensemble, tiles, tile_live, observed, perturb, obs_var)


def solution(mesh):
    return jax.shard_map(
        on_device,
        mesh=mesh,
        in_specs=(
            P(("region", "group"), None),
            P(None, None, ("region", "group")),
            P(),
            P(),
            P(),
            P(),
        ),
        out_specs=P(("region", "group"), None),
        check_vma=False,
    )
```
